32 devices in a mesh: row: 8 (over z, core), vec: 4 (over y, x).
Axes of the slice: x: 2, y: 2, z: 4, core: 2. Of those that a mesh axis runs over, the one named last changes fastest.
Arguments:
- vectors: float32 [8192, 512], P('row', 'vec'), may hold values from -6 to 6
- reflectors: float32 [3, 8192, 512], P(None, ('row', 'vec')), may hold values from -0.0625 to 0.0625
- triangles: float32 [3, 512, 512], P(None, None, 'vec'), may hold values from -0.04 to 2, as said below
Outputs:
- transformed: float32 [8192, 512], P('row', 'vec')
The draws below stay inside these ranges and needn't reach their ends.
Inputs may be any that keep to these rules, and one draw needn't show every extreme that they name: Each triangles[k] is upper triangular with a diagonal between 0.5 and 2.
All inputs are finite; a program needn't handle non-finite values.
Results may differ from the reference program's by a relative error of at most 0.0001.
Values sent between devices are 32-bit elements; how exact they have to be, the bound alone decides.
No kernel may reach another device: no remote copies, remote signals or barrier semaphores. Data moves between devices by JAX's collectives and lax.ppermute only.
A program may use at most 64 MiB of HBM per device.

```python
import jax
import jax.numpy as jnp
from jax import lax

B = 512
PANELS = 3
ROWS = 8192
EIGS = 512


def draw_triangles(key, part):
    first, second = jax.random.split(jax.random.fold_in(key, 11))
    upper = jax.random.uniform(first, (PANELS, B, B), jnp.float32, -0.04, 0.04)
    diagonal = jax.random.uniform(second, (PANELS, B), jnp.float32, 1.0, 2.0)
    rowsidx = lax.broadcasted_iota(jnp.int32, (B, B), 0)
    colsidx = lax.broadcasted_iota(jnp.int32, (B, B), 1)
    return jnp.where(rowsidx == colsidx, diagonal[:, :, None], jnp.where(colsidx > rowsidx, upper, 0.0))


def block_scale(own_key, shape, cuts, least, largest):
    factor_of = 1.0
    for axis_at, blocks in cuts:
        heights = jax.random.uniform(jax.random.fold_in(jax.random.fold_in(own_key, 6), axis_at), (blocks,), jnp.float32, least / len(cuts), largest / len(cuts))
        factor_of = factor_of * jnp.repeat(jnp.exp(heights), shape[axis_at] // blocks).reshape((-1,) + (1,) * (len(shape) - 1 - axis_at))
    return factor_of


def gaussian(stream_key, extent, deviation, bound, pieces=(), dtype=jnp.bfloat16):
    drawn = jax.random.normal(stream_key, extent, jnp.float32) * deviation
    if len(pieces) > 0:
        drawn = block_scale(stream_key, extent, pieces, -0.22, 0.18) * drawn
    return jnp.clip(drawn, min=-bound, max=bound).astype(dtype)


def setup_inputs(seed: int = 0) -> dict:
    seeds = jax.random.split(jax.random.key(seed), 4)
    vectors = gaussian(seeds[0], (ROWS, EIGS), 1.0, 6.0, ((0, 8), (1, 4)), jnp.float32)
    reflectors = gaussian(seeds[1], (PANELS, ROWS, B), ROWS ** -0.5, 0.0625, ((1, 32),), jnp.float32)
    triangles = draw_triangles(jax.random.fold_in(seeds[3], 71), 0)
    return {"vectors": vectors, "reflectors": reflectors, "triangles": triangles}


def reference(vectors, reflectors, triangles):
    highest = lax.Precision.HIGHEST
    current = vectors
    for step in range(PANELS):
        panel = PANELS - 1 - step
        section = reflectors[panel]
        projected = lax.dot_general(section, current, (((0,), (0,)), ((), ())), precision=highest, preferred_element_type=jnp.float32)
        coefficients = jnp.dot(triangles[panel], projected, precision=highest, preferred_element_type=jnp.float32)
        current = current - jnp.dot(section, coefficients, precision=highest, preferred_element_type=jnp.float32)
    return current
```

```python
import functools

import jax
import jax.numpy as jnp
from jax import lax
from jax.experimental import pallas as pl
from jax.experimental.pallas import tpu as pltpu
from jax.sharding import Mesh, PartitionSpec as P

F32, BF16 = jnp.float32, jnp.bfloat16
NN = (((1,), (0,)), ((), ()))
NT = (((1,), (1,)), ((), ()))


def split(a):
    head = a.astype(BF16)
    return head, (a - head.astype(F32)).astype(BF16)


def dot3(a, b, dims):
    (ah, al), (bh, bl) = split(a), split(b)
    one = functools.partial(lax.dot_general, dimension_numbers=dims, preferred_element_type=F32)
    return one(ah, bh) + (one(ah, bl) + one(al, bh))


def place():
    return lax.axis_index("y") * 2 + lax.axis_index("x"), lax.axis_index("core")


def blocks_of(refs, width):
    own, along_x, along_y, low, high = refs
    rows = own.shape[-2]
    half = rows // 2
    return [
        (0, 0, rows, own),
        (1, 0, rows, along_x),
        (2, 0, rows, along_y),
        (3, 0, half, low),
        (3, half, half, high),
    ]


def window(place_v, block, first, size, rows):
    return pl.ds(pl.multiple_of((place_v ^ block) * rows + first, 8), size)


def project(total, current, refs, v, width):
    rows = refs[0].shape[-2]
    for block, first, size, ref in blocks_of(refs, width):
        x = current[window(v, block, first, size, rows), :]
        part = dot3(x.T, ref[:, :width], NN)
        total = part if total is None else total + part
    return total


def give_out(total, core, keep, send):
    half = keep.shape[0]
    mine = core == 0
    keep[...] = jnp.where(mine, total[:half], total[half:])
    send[...] = jnp.where(mine, total[half:], total[:half])


def first_kernel(width, x, *refs):
    v, core = place()
    refs, (keep, send) = refs[:5], refs[5:]
    give_out(project(None, x, refs, v, width), core, keep, send)


def both_halves(mine, other, core):
    a, b = mine[...], other[...]
    first = core == 0
    return jnp.concatenate([jnp.where(first, a, b), jnp.where(first, b, a)], axis=0)


def update(current, out, refs, coefficients, v, width):
    rows = refs[0].shape[-2]
    for block, first, size, ref in blocks_of(refs, width):
        at = window(v, block, first, size, rows)
        out[at, :] = current[at, :] - dot3(ref[:, :width], coefficients, NT)


def middle_kernel(width, x, mine, other, *refs):
    v, core = place()
    old, new, (out, keep, send) = refs[:5], refs[5:10], refs[10:]
    update(x, out, old, both_halves(mine, other, core), v, width)
    give_out(project(None, out, new, v, width), core, keep, send)


def last_kernel(width, x, mine, other, *refs):
    v, core = place()
    update(x, refs[5], refs[:5], both_halves(mine, other, core), v, width)


def solve_kernel(panel, column, s, r1, r2, r3, factor, exchanged, along_x, along_y, low, high, out):
    v, core = place()
    total = (s[...] + r1[...]) + (r2[...] + r3[...])
    share = factor.shape[-1]
    half = factor.shape[-2] // 2
    at = pl.ds(column, share)
    ex = exchanged.shape[-1] // 3
    mine = [
        factor[panel, pl.ds(pl.multiple_of(core * half, 8), half), :],
        along_x[:, at],
        along_y[:, at],
        jnp.concatenate([low[:, at], high[:, at]], axis=0),
    ]
    other = [factor[panel, pl.ds(pl.multiple_of((1 - core) * half, 8), half), :]]
    other += [exchanged[:, i * ex : i * ex + share] for i in range(3)]
    sums = [None, None]
    parts = split_columns(total, v, share)
    for block in range(4):
        for i, t in enumerate((mine[block], other[block])):
            part = dot3(parts[block], t, NT)
            sums[i] = part if sums[i] is None else sums[i] + part
    out[...] = jnp.where(core == 0, jnp.concatenate(sums, axis=1), jnp.concatenate(sums[::-1], axis=1))


def split_columns(total, v, share):
    b = [total[:, i * share : (i + 1) * share] for i in range(4)]
    odd, up = (v & 1) == 1, (v & 2) == 2
    p, q = jnp.where(odd, b[1], b[0]), jnp.where(odd, b[0], b[1])
    r, s = jnp.where(odd, b[3], b[2]), jnp.where(odd, b[2], b[3])
    return [jnp.where(up, r, p), jnp.where(up, s, q), jnp.where(up, p, r), jnp.where(up, q, s)]


def vmem(n):
    return [pl.BlockSpec(memory_space=pltpu.VMEM)] * n


def call(kernel, outs, args, flops, name):
    nbytes = sum(4 * a.size for a in args) + sum(4 * o.size for o in outs)
    return pl.pallas_call(
        kernel,
        out_shape=outs,
        in_specs=vmem(len(args)),
        out_specs=vmem(len(outs)),
        name=name,
        cost_estimate=pl.CostEstimate(flops=flops, bytes_accessed=nbytes, transcendentals=0),
    )(*args)


def swap(a, axis, by=1):
    n = lax.axis_size(axis)
    return lax.ppermute(a, axis, [(i, i ^ by) for i in range(n)])


def gather(pack):
    half = pack.shape[0] // 2
    along_x, along_y = swap(pack, "x"), swap(pack, "y")
    return pack, along_x, along_y, swap(along_y[:half], "x"), swap(along_x[half:], "y")


def fast(vectors, reflectors, triangles):
    rows, share = vectors.shape
    panels, own_rows, width = reflectors.shape
    core = lax.axis_index("core")
    half = width // 2
    part = jax.ShapeDtypeStruct((share // 2, width), F32)
    whole = jax.ShapeDtypeStruct((rows, share), F32)
    work = 2 * rows * width * share

    def factor_half(panel):
        return lax.dynamic_slice(triangles[panel], (core * half, 0), (half, share))

    riders = {panels - 1: []}
    for panel in range(panels - 1):
        riders[panel] = [panel + 1]
    riders[0] = riders[0] + [0]
    sections, factors = {}, {}
    for panel in reversed(range(panels)):
        pack = jnp.concatenate([reflectors[panel]] + [factor_half(r) for r in riders[panel]], axis=1)
        sections[panel] = gather(pack)
        received = sections[panel][1:]
        for i, r in enumerate(riders[panel]):
            at = width + i * share
            cut = [a[:, at : at + share] for a in received]
            mine = jnp.concatenate([cut[0], cut[1], jnp.concatenate(cut[2:], axis=0)], axis=1)
            factors[r] = (at, swap(mine, "core"), received)

    def reduced(keep, send, panel):
        s = keep + swap(send, "core")
        r = [swap(s, "z", by) for by in (1, 2, 3)]
        at, exchanged, received = factors[panel]
        mine = call(
            functools.partial(solve_kernel, panel, at),
            [part],
            [s, *r, triangles, exchanged, *received],
            2 * width * width * share // 2,
            "solve",
        )[0]
        return mine, swap(mine, "core")

    top = panels - 1
    keep, send = call(functools.partial(first_kernel, width), [part, part], [vectors, *sections[top]], work, "first")
    current = vectors
    for panel in reversed(range(1, panels)):
        c = reduced(keep, send, panel)
        current, keep, send = call(
            functools.partial(middle_kernel, width),
            [whole, part, part],
            [current, *c, *sections[panel], *sections[panel - 1]],
            2 * work,
            "middle",
        )
    c = reduced(keep, send, 0)
    return call(functools.partial(last_kernel, width), [whole], [current, *c, *sections[0]], work, "last")[0]


def general(vectors, reflectors, triangles):
    highest = lax.Precision.HIGHEST
    row, vec = ("z", "core"), ("y", "x")
    current = vectors
    for panel in reversed(range(reflectors.shape[0])):
        section = lax.all_gather(reflectors[panel], vec, axis=0, tiled=True)
        factor = lax.all_gather(triangles[panel], vec, axis=1, tiled=True)
        partial_value = lax.dot_general(
            section, current, (((0,), (0,)), ((), ())), precision=highest, preferred_element_type=F32
        )
        share = lax.psum_scatter(partial_value, row, scatter_dimension=1, tiled=True)
        owned = jnp.dot(factor, share, precision=highest, preferred_element_type=F32)
        coefficients = lax.all_gather(owned, row, axis=1, tiled=True)
        current = current - jnp.dot(section, coefficients, precision=highest, preferred_element_type=F32)
    return current


def solution(mesh):
    rows, vecs = mesh.shape["row"], mesh.shape["vec"]
    side = next(s for s in range(int(vecs**0.5), 0, -1) if vecs % s == 0)
    cores = 2 if rows % 2 == 0 else 1
    fine = Mesh(mesh.devices.reshape(rows // cores, cores, side, vecs // side), ("z", "core", "y", "x"))
    small = fine.devices.shape == (4, 2, 2, 2)
    row, vec = ("z", "core"), ("y", "x")
    return jax.shard_map(
        fast if small else general,
        mesh=fine,
        in_specs=(P(row, vec), P(None, row + vec, None), P(None, None, vec)),
        out_specs=P(row, vec),
        check_vma=False,
    )
```

```python
import functools

import jax
import jax.numpy as jnp
from jax import lax
from jax.experimental import pallas as pl
from jax.experimental.pallas import tpu as pltpu
from jax.sharding import Mesh, PartitionSpec as P


F32, BF16 = jnp.float32, jnp.bfloat16
NN = (((1,), (0,)), ((), ()))
NT = (((1,), (1,)), ((), ()))


def split(a):
    head = a.astype(BF16)
    return head, (a - head.astype(F32)).astype(BF16)


def dot3(a, b, dims):
    (ah, al), (bh, bl) = split(a), split(b)
    one = functools.partial(lax.dot_general, dimension_numbers=dims, preferred_element_type=F32)
    return one(ah, bh) + (one(ah, bl) + one(al, bh))


def place():
    return lax.axis_index("y") * 2 + lax.axis_index("x"), lax.axis_index("core")


def blocks_of(refs):
    own, along_x, along_y, low, high = refs
    rows = own.shape[-2]
    half = rows // 2
    return [
        (0, 0, rows, own),
        (1, 0, rows, along_x),
        (2, 0, rows, along_y),
        (3, 0, half, low),
        (3, half, half, high),
    ]


def window(place_v, block, first, size, rows):
    return pl.ds(pl.multiple_of((place_v ^ block) * rows + first, 8), size)


def project(total, current, refs, v, width):
    rows = refs[0].shape[-2]
    for block, first, size, ref in blocks_of(refs):
        x = current[window(v, block, first, size, rows), :]
        part = dot3(x.T, ref[:, :width], NN)
        total = part if total is None else total + part
    return total


def give_out(total, core, keep, send):
    half = keep.shape[0]
    mine = core == 0
    keep[...] = jnp.where(mine, total[:half], total[half:])
    send[...] = jnp.where(mine, total[half:], total[:half])


def first_kernel(width, x, *refs):
    v, core = place()
    refs, (keep, send) = refs[:5], refs[5:]
    give_out(project(None, x, refs, v, width), core, keep, send)


def both_halves(mine, other, core):
    a, b = mine[...], other[...]
    first = core == 0
    return jnp.concatenate([jnp.where(first, a, b), jnp.where(first, b, a)], axis=0)


def update(current, out, refs, coefficients, v, width):
    rows = refs[0].shape[-2]
    for block, first, size, ref in blocks_of(refs):
        at = window(v, block, first, size, rows)
        out[at, :] = current[at, :] - dot3(ref[:, :width], coefficients, NT)


def middle_kernel(width, x, mine, other, *refs):
    v, core = place()
    old, new, (out, keep, send) = refs[:5], refs[5:10], refs[10:]
    update(x, out, old, both_halves(mine, other, core), v, width)
    give_out(project(None, out, new, v, width), core, keep, send)


def last_kernel(width, x, mine, other, *refs):
    v, core = place()
    update(x, refs[5], refs[:5], both_halves(mine, other, core), v, width)


def solve_kernel(panel, column, s, r1, r2, r3, factor, exchanged, along_x, along_y, low, high, out):
    v, core = place()
    total = (s[...] + r1[...]) + (r2[...] + r3[...])
    share = factor.shape[-1]
    half = factor.shape[-2] // 2
    at = pl.ds(column, share)
    ex = exchanged.shape[-1] // 3
    mine = [
        factor[panel, pl.ds(pl.multiple_of(core * half, 8), half), :],
        along_x[:, at],
        along_y[:, at],
        jnp.concatenate([low[:, at], high[:, at]], axis=0),
    ]
    other = [factor[panel, pl.ds(pl.multiple_of((1 - core) * half, 8), half), :]]
    other += [exchanged[:, i * ex : i * ex + share] for i in range(3)]
    sums = [None, None]
    parts = split_columns(total, v, share)
    for block in range(4):
        for i, t in enumerate((mine[block], other[block])):
            part = dot3(parts[block], t, NT)
            sums[i] = part if sums[i] is None else sums[i] + part
    out[...] = jnp.where(core == 0, jnp.concatenate(sums, axis=1), jnp.concatenate(sums[::-1], axis=1))


def split_columns(total, v, share):
    b = [total[:, i * share : (i + 1) * share] for i in range(4)]
    odd, up = (v & 1) == 1, (v & 2) == 2
    p, q = jnp.where(odd, b[1], b[0]), jnp.where(odd, b[0], b[1])
    r, s = jnp.where(odd, b[3], b[2]), jnp.where(odd, b[2], b[3])
    return [jnp.where(up, r, p), jnp.where(up, s, q), jnp.where(up, p, r), jnp.where(up, q, s)]


def vmem(n):
    return [pl.BlockSpec(memory_space=pltpu.VMEM)] * n


def call(kernel, outs, args, flops):
    nbytes = sum(4 * a.size for a in args) + sum(4 * o.size for o in outs)
    return pl.pallas_call(
        kernel,
        out_shape=outs,
        in_specs=vmem(len(args)),
        out_specs=vmem(len(outs)),
        compiler_params=pltpu.CompilerParams(vmem_limit_bytes=12 * 2**20),
        cost_estimate=pl.CostEstimate(flops=flops, bytes_accessed=nbytes, transcendentals=0),
    )(*args)


def swap(a, axis, by=1):
    n = lax.axis_size(axis)
    return lax.ppermute(a, axis, [(i, i ^ by) for i in range(n)])


def gather(pack):
    half = pack.shape[0] // 2
    along_x, along_y = swap(pack, "x"), swap(pack, "y")
    low, high = swap(along_y[:half], "x"), swap(along_x[half:], "y")
    return pack, along_x, along_y, low, high


def fast(vectors, reflectors, triangles):
    rows, share = vectors.shape
    panels, _, width = reflectors.shape
    core = lax.axis_index("core")
    half = width // 2
    part = jax.ShapeDtypeStruct((share // 2, width), F32)
    whole = jax.ShapeDtypeStruct((rows, share), F32)
    work = 2 * rows * width * share

    def factor_half(panel):
        return lax.dynamic_slice(triangles[panel], (core * half, 0), (half, share))

    riders = {panels - 1: []}
    for panel in range(panels - 1):
        riders[panel] = [panel + 1]
    riders[0] = riders[0] + [0]
    sections, factors = {}, {}
    for panel in reversed(range(panels)):
        pack = jnp.concatenate([reflectors[panel]] + [factor_half(r) for r in riders[panel]], axis=1)
        sections[panel] = gather(pack)
        if panel == panels - 1:
            along_x, reflectors, triangles = lax.optimization_barrier((sections[panel][1], reflectors, triangles))
            sections[panel] = (pack, along_x, *sections[panel][2:])
        received = sections[panel][1:]
        for i, r in enumerate(riders[panel]):
            at = width + i * share
            cut = [a[:, at : at + share] for a in received]
            mine = jnp.concatenate([cut[0], cut[1], jnp.concatenate(cut[2:], axis=0)], axis=1)
            factors[r] = (at, swap(mine, "core"), received)

    def reduced(keep, send, panel):
        s = keep + swap(send, "core")
        r = [swap(s, "z", by) for by in (1, 2, 3)]
        at, exchanged, received = factors[panel]
        mine = call(
            functools.partial(solve_kernel, panel, at),
            [part],
            [s, *r, triangles, exchanged, *received],
            2 * width * width * share // 2,
        )[0]
        return mine, swap(mine, "core")

    top = panels - 1
    keep, send = call(functools.partial(first_kernel, width), [part, part], [vectors, *sections[top]], work)
    current = vectors
    for panel in reversed(range(1, panels)):
        c = reduced(keep, send, panel)
        current, keep, send = call(
            functools.partial(middle_kernel, width),
            [whole, part, part],
            [current, *c, *sections[panel], *sections[panel - 1]],
            2 * work,
        )
    c = reduced(keep, send, 0)
    return call(functools.partial(last_kernel, width), [whole], [current, *c, *sections[0]], work)[0]


def general(vectors, reflectors, triangles):
    highest = lax.Precision.HIGHEST
    row, vec = ("z", "core"), ("y", "x")
    current = vectors
    for panel in reversed(range(reflectors.shape[0])):
        section = lax.all_gather(reflectors[panel], vec, axis=0, tiled=True)
        factor = lax.all_gather(triangles[panel], vec, axis=1, tiled=True)
        partial_value = lax.dot_general(
            section, current, (((0,), (0,)), ((), ())), precision=highest, preferred_element_type=F32
        )
        share = lax.psum_scatter(partial_value, row, scatter_dimension=1, tiled=True)
        owned = jnp.dot(factor, share, precision=highest, preferred_element_type=F32)
        coefficients = lax.all_gather(owned, row, axis=1, tiled=True)
        current = current - jnp.dot(section, coefficients, precision=highest, preferred_element_type=F32)
    return current


def solution(mesh):
    rows, vecs = mesh.shape["row"], mesh.shape["vec"]
    side = next(s for s in range(int(vecs**0.5), 0, -1) if vecs % s == 0)
    cores = 2 if rows % 2 == 0 else 1
    fine = Mesh(mesh.devices.reshape(rows // cores, cores, side, vecs // side), ("z", "core", "y", "x"))
    small = fine.devices.shape == (4, 2, 2, 2)
    row, vec = ("z", "core"), ("y", "x")

    def body(*args):
        return (fast if small else general)(*args)

    return jax.shard_map(
        body,
        mesh=fine,
        in_specs=(P(row, vec), P(None, row + vec, None), P(None, None, vec)),
        out_specs=P(row, vec),
        check_vma=False,
    )
```

```python
import functools

import jax
import jax.numpy as jnp
from jax import lax
from jax.experimental import pallas as pl
from jax.experimental.pallas import tpu as pltpu
from jax.sharding import Mesh, PartitionSpec as P


F32, BF16 = jnp.float32, jnp.bfloat16
NN = (((1,), (0,)), ((), ()))
NT = (((1,), (1,)), ((), ()))
PIECES = 8


def split(a):
    head = a.astype(BF16)
    return head, (a - head.astype(F32)).astype(BF16)


def dot3(a, b, dims):
    (ah, al), (bh, bl) = split(a), split(b)
    one = functools.partial(lax.dot_general, dimension_numbers=dims, preferred_element_type=F32)
    return one(ah, bh) + (one(ah, bl) + one(al, bh))


def place():
    return lax.axis_index("y") * 2 + lax.axis_index("x"), lax.axis_index("core")


def blocks_of(refs):
    size = refs[0].shape[0]
    return [(i // 2, i % 2 * size, ref) for i, ref in enumerate(refs)]


def window(v, block, first, size):
    return pl.ds(pl.multiple_of((v ^ block) * 2 * size + first, 8), size)


def project(current, refs, v):
    total = None
    for block, first, ref in blocks_of(refs):
        x = current[window(v, block, first, ref.shape[0]), :]
        part = dot3(x.T, ref[...], NN)
        total = part if total is None else total + part
    return total


def give_out(total, core, keep, send):
    half = keep.shape[0]
    mine = core == 0
    keep[...] = jnp.where(mine, total[:half], total[half:])
    send[...] = jnp.where(mine, total[half:], total[:half])


def first_kernel(x, *refs):
    v, core = place()
    refs, (keep, send) = refs[:PIECES], refs[PIECES:]
    give_out(project(x, refs, v), core, keep, send)


def both_halves(mine, other, core):
    a, b = mine[...], other[...]
    first = core == 0
    return jnp.concatenate([jnp.where(first, a, b), jnp.where(first, b, a)], axis=0)


def update(current, out, refs, coefficients, v):
    for block, first, ref in blocks_of(refs):
        at = window(v, block, first, ref.shape[0])
        out[at, :] = current[at, :] - dot3(ref[...], coefficients, NT)


def middle_kernel(x, mine, other, *refs):
    v, core = place()
    old, new, (out, keep, send) = refs[:PIECES], refs[PIECES : 2 * PIECES], refs[2 * PIECES :]
    update(x, out, old, both_halves(mine, other, core), v)
    give_out(project(out, new, v), core, keep, send)


def last_kernel(x, mine, other, *refs):
    v, core = place()
    update(x, refs[PIECES], refs[:PIECES], both_halves(mine, other, core), v)


def solve_kernel(panel, n, *refs):
    v, core = place()
    total = refs[0][...]
    for i in range(1, n):
        total = total + refs[i][...]
    factor, exchanged, *mine = refs[n:-1]
    out = refs[-1]
    share = factor.shape[-1]
    half = factor.shape[-2] // 2
    mine = [factor[panel, pl.ds(pl.multiple_of(core * half, 8), half), :]] + [a[...] for a in mine]
    other = [factor[panel, pl.ds(pl.multiple_of((1 - core) * half, 8), half), :]]
    other += [exchanged[:, i * share : (i + 1) * share] for i in range(3)]
    sums = [None, None]
    parts = split_columns(total, v, share)
    for block in range(4):
        for i, t in enumerate((mine[block], other[block])):
            part = dot3(parts[block], t, NT)
            sums[i] = part if sums[i] is None else sums[i] + part
    out[...] = jnp.where(core == 0, jnp.concatenate(sums, axis=1), jnp.concatenate(sums[::-1], axis=1))


def split_columns(total, v, share):
    b = [total[:, i * share : (i + 1) * share] for i in range(4)]
    odd, up = (v & 1) == 1, (v & 2) == 2
    p, q = jnp.where(odd, b[1], b[0]), jnp.where(odd, b[0], b[1])
    r, s = jnp.where(odd, b[3], b[2]), jnp.where(odd, b[2], b[3])
    return [jnp.where(up, r, p), jnp.where(up, s, q), jnp.where(up, p, r), jnp.where(up, q, s)]


def vmem(n):
    return [pl.BlockSpec(memory_space=pltpu.VMEM)] * n


def call(kernel, outs, args, flops):
    nbytes = sum(4 * a.size for a in args) + sum(4 * o.size for o in outs)
    return pl.pallas_call(
        kernel,
        out_shape=outs,
        in_specs=vmem(len(args)),
        out_specs=vmem(len(outs)),
        compiler_params=pltpu.CompilerParams(vmem_limit_bytes=12 * 2**20),
        cost_estimate=pl.CostEstimate(flops=flops, bytes_accessed=nbytes, transcendentals=0),
    )(*args)


def swap(a, axis, by=1):
    n = lax.axis_size(axis)
    return lax.ppermute(a, axis, [(i, i ^ by) for i in range(n)])


def gather(block):
    half = block.shape[0] // 2
    a, b = block[:half], block[half:]
    ya, xb = swap(a, "y"), swap(b, "x")
    xa, yb = swap(a, "x"), swap(b, "y")
    return a, b, xa, xb, ya, yb, swap(ya, "x"), swap(xb, "y")


def cross(a):
    return lax.ppermute(a, ("y", "x"), [(i, i ^ 3) for i in range(4)])


def fast(vectors, reflectors, triangles):
    rows, share = vectors.shape
    panels, _, width = reflectors.shape
    core, sums = lax.axis_index("core"), lax.axis_size("z")
    half = width // 2
    part = jax.ShapeDtypeStruct((share // 2, width), F32)
    whole = jax.ShapeDtypeStruct((rows, share), F32)
    work = 2 * rows * width * share
    top = panels - 1

    sections, factors = {}, {}
    for k in reversed(range(panels)):
        sections[k] = gather(reflectors[k])
        own = lax.dynamic_slice(triangles[k], (core * half, 0), (half, share))
        received = swap(own, "x"), swap(own, "y"), cross(own)
        factors[k] = (swap(jnp.concatenate(received, axis=1), "core"), *received)
        if k == top:
            pieces = list(sections[k])
            pieces[4], reflectors, triangles = lax.optimization_barrier((pieces[4], reflectors, triangles))
            sections[k] = tuple(pieces)

    def reduced(keep, send, k):
        s = keep + swap(send, "core")
        r = [swap(s, "z", by) for by in range(1, sums)]
        mine = call(
            functools.partial(solve_kernel, k, sums), [part], [s, *r, triangles, *factors[k]], width * width * share
        )[0]
        return mine, swap(mine, "core")

    keep, send = call(first_kernel, [part, part], [vectors, *sections[top]], work)
    current = vectors
    for k in reversed(range(1, panels)):
        c = reduced(keep, send, k)
        current, keep, send = call(
            middle_kernel, [whole, part, part], [current, *c, *sections[k], *sections[k - 1]], 2 * work
        )
    c = reduced(keep, send, 0)
    return call(last_kernel, [whole], [current, *c, *sections[0]], work)[0]


def general(vectors, reflectors, triangles):
    highest = lax.Precision.HIGHEST
    row, vec = ("z", "core"), ("y", "x")
    current = vectors
    for panel in reversed(range(reflectors.shape[0])):
        section = lax.all_gather(reflectors[panel], vec, axis=0, tiled=True)
        factor = lax.all_gather(triangles[panel], vec, axis=1, tiled=True)
        partial_value = lax.dot_general(
            section, current, (((0,), (0,)), ((), ())), precision=highest, preferred_element_type=F32
        )
        share = lax.psum_scatter(partial_value, row, scatter_dimension=1, tiled=True)
        owned = jnp.dot(factor, share, precision=highest, preferred_element_type=F32)
        coefficients = lax.all_gather(owned, row, axis=1, tiled=True)
        current = current - jnp.dot(section, coefficients, precision=highest, preferred_element_type=F32)
    return current


def solution(mesh):
    rows, vecs = mesh.shape["row"], mesh.shape["vec"]
    side = next(s for s in range(int(vecs**0.5), 0, -1) if vecs % s == 0)
    cores = 2 if rows % 2 == 0 else 1
    fine = Mesh(mesh.devices.reshape(rows // cores, cores, side, vecs // side), ("z", "core", "y", "x"))
    halves = [fine.shape[axis] == 2 for axis in ("core", "y", "x")]
    small = all(halves) and fine.shape["z"] & (fine.shape["z"] - 1) == 0
    row, vec = ("z", "core"), ("y", "x")

    def body(*args):
        return (fast if small else general)(*args)

    return jax.shard_map(
        body,
        mesh=fine,
        in_specs=(P(row, vec), P(None, row + vec, None), P(None, None, vec)),
        out_specs=P(row, vec),
        check_vma=False,
    )
```

```python
import functools

import jax
import jax.numpy as jnp
from jax import lax
from jax.experimental import pallas as pl
from jax.experimental.pallas import tpu as pltpu
from jax.sharding import Mesh, PartitionSpec as P


F32, BF16 = jnp.float32, jnp.bfloat16
NN = (((1,), (0,)), ((), ()))
NT = (((1,), (1,)), ((), ()))
PIECES = 8


def split(a):
    head = a.astype(BF16)
    return head, (a - head.astype(F32)).astype(BF16)


def dot3(a, b, dims):
    (ah, al), (bh, bl) = split(a), split(b)
    one = functools.partial(lax.dot_general, dimension_numbers=dims, preferred_element_type=F32)
    return one(ah, bh) + (one(ah, bl) + one(al, bh))


def place():
    return lax.axis_index("y") * 2 + lax.axis_index("x"), lax.axis_index("core")


def blocks_of(refs, skip=0):
    size = refs[0].shape[0]
    return [(i // 2, i % 2 * size, ref) for i, ref in enumerate(refs, skip)]


def window(v, block, first, size):
    return pl.ds(pl.multiple_of((v ^ block) * 2 * size + first, 8), size)


def project(current, refs, v, skip=0):
    total = None
    for block, first, ref in blocks_of(refs, skip):
        x = current[window(v, block, first, ref.shape[0]), :]
        part = dot3(x.T, ref[...], NN)
        total = part if total is None else total + part
    return total


def give_out(total, core, keep, send):
    half = keep.shape[0]
    mine = core == 0
    keep[...] = jnp.where(mine, total[:half], total[half:])
    send[...] = jnp.where(mine, total[half:], total[:half])


def early_kernel(x, *refs):
    v, _ = place()
    refs[-1][...] = project(x, refs[:-1], v)


def late_kernel(x, total, *refs):
    v, core = place()
    refs, (keep, send) = refs[:-2], refs[-2:]
    give_out(total[...] + project(x, refs, v, PIECES - len(refs)), core, keep, send)


def both_halves(mine, other, core):
    a, b = mine[...], other[...]
    first = core == 0
    return jnp.concatenate([jnp.where(first, a, b), jnp.where(first, b, a)], axis=0)


def update(current, out, refs, coefficients, v):
    for block, first, ref in blocks_of(refs):
        at = window(v, block, first, ref.shape[0])
        out[at, :] = current[at, :] - dot3(ref[...], coefficients, NT)


def middle_kernel(x, mine, other, *refs):
    v, core = place()
    old, new, (out, keep, send) = refs[:PIECES], refs[PIECES : 2 * PIECES], refs[2 * PIECES :]
    update(x, out, old, both_halves(mine, other, core), v)
    give_out(project(out, new, v), core, keep, send)


def last_kernel(x, mine, other, *refs):
    v, core = place()
    update(x, refs[PIECES], refs[:PIECES], both_halves(mine, other, core), v)


def solve_kernel(panel, n, *refs):
    v, core = place()
    total = refs[0][...]
    for i in range(1, n):
        total = total + refs[i][...]
    factor, exchanged, *mine = refs[n:-1]
    out = refs[-1]
    share = factor.shape[-1]
    half = factor.shape[-2] // 2
    mine = [factor[panel, pl.ds(pl.multiple_of(core * half, 8), half), :]] + [a[...] for a in mine]
    other = [factor[panel, pl.ds(pl.multiple_of((1 - core) * half, 8), half), :]]
    other += [exchanged[:, i * share : (i + 1) * share] for i in range(3)]
    sums = [None, None]
    parts = split_columns(total, v, share)
    for block in range(4):
        for i, t in enumerate((mine[block], other[block])):
            part = dot3(parts[block], t, NT)
            sums[i] = part if sums[i] is None else sums[i] + part
    out[...] = jnp.where(core == 0, jnp.concatenate(sums, axis=1), jnp.concatenate(sums[::-1], axis=1))


def split_columns(total, v, share):
    b = [total[:, i * share : (i + 1) * share] for i in range(4)]
    odd, up = (v & 1) == 1, (v & 2) == 2
    p, q = jnp.where(odd, b[1], b[0]), jnp.where(odd, b[0], b[1])
    r, s = jnp.where(odd, b[3], b[2]), jnp.where(odd, b[2], b[3])
    return [jnp.where(up, r, p), jnp.where(up, s, q), jnp.where(up, p, r), jnp.where(up, q, s)]


def vmem(n):
    return [pl.BlockSpec(memory_space=pltpu.VMEM)] * n


def call(kernel, outs, args, flops):
    nbytes = sum(4 * a.size for a in args) + sum(4 * o.size for o in outs)
    return pl.pallas_call(
        kernel,
        out_shape=outs,
        in_specs=vmem(len(args)),
        out_specs=vmem(len(outs)),
        compiler_params=pltpu.CompilerParams(vmem_limit_bytes=12 * 2**20),
        cost_estimate=pl.CostEstimate(flops=flops, bytes_accessed=nbytes, transcendentals=0),
    )(*args)


def swap(a, axis, by=1):
    n = lax.axis_size(axis)
    return lax.ppermute(a, axis, [(i, i ^ by) for i in range(n)])


def gather(block):
    half = block.shape[0] // 2
    a, b = block[:half], block[half:]
    ya, xb = swap(a, "y"), swap(b, "x")
    xa, yb = swap(a, "x"), swap(b, "y")
    return a, b, xa, xb, ya, yb, swap(ya, "x"), swap(xb, "y")


def cross(a):
    return lax.ppermute(a, ("y", "x"), [(i, i ^ 3) for i in range(4)])


def fast(vectors, reflectors, triangles):
    rows, share = vectors.shape
    panels, _, width = reflectors.shape
    core, sums = lax.axis_index("core"), lax.axis_size("z")
    half = width // 2
    part = jax.ShapeDtypeStruct((share // 2, width), F32)
    whole = jax.ShapeDtypeStruct((rows, share), F32)
    work = 2 * rows * width * share
    top = panels - 1

    sections, factors = {}, {}
    for k in reversed(range(panels)):
        sections[k] = gather(reflectors[k])
        own = lax.dynamic_slice(triangles[k], (core * half, 0), (half, share))
        received = swap(own, "x"), swap(own, "y"), cross(own)
        joined = jnp.concatenate(received, axis=1)
        factors[k] = (swap(joined, "core"), *received)
        if k == top:
            pieces = list(sections[k])
            pieces[4], reflectors, triangles = lax.optimization_barrier((pieces[4], reflectors, triangles))
            sections[k] = tuple(pieces)

    def reduced(keep, send, k):
        s = keep + swap(send, "core")
        r = [swap(s, "z", by) for by in range(1, sums)]
        mine = call(
            functools.partial(solve_kernel, k, sums), [part], [s, *r, triangles, *factors[k]], width * width * share
        )[0]
        return mine, swap(mine, "core")

    early, late = sections[top][:-2], sections[top][-2:]
    total = call(early_kernel, [jax.ShapeDtypeStruct((share, width), F32)], [vectors, *early], work * 3 // 4)[0]
    keep, send = call(late_kernel, [part, part], [vectors, total, *late], work // 4)
    current = vectors
    for k in reversed(range(1, panels)):
        c = reduced(keep, send, k)
        current, keep, send = call(
            middle_kernel, [whole, part, part], [current, *c, *sections[k], *sections[k - 1]], 2 * work
        )
    c = reduced(keep, send, 0)
    return call(last_kernel, [whole], [current, *c, *sections[0]], work)[0]


def general(vectors, reflectors, triangles):
    highest = lax.Precision.HIGHEST
    row, vec = ("z", "core"), ("y", "x")
    current = vectors
    for panel in reversed(range(reflectors.shape[0])):
        section = lax.all_gather(reflectors[panel], vec, axis=0, tiled=True)
        factor = lax.all_gather(triangles[panel], vec, axis=1, tiled=True)
        partial_value = lax.dot_general(
            section, current, (((0,), (0,)), ((), ())), precision=highest, preferred_element_type=F32
        )
        share = lax.psum_scatter(partial_value, row, scatter_dimension=1, tiled=True)
        owned = jnp.dot(factor, share, precision=highest, preferred_element_type=F32)
        coefficients = lax.all_gather(owned, row, axis=1, tiled=True)
        current = current - jnp.dot(section, coefficients, precision=highest, preferred_element_type=F32)
    return current


def solution(mesh):
    rows, vecs = mesh.shape["row"], mesh.shape["vec"]
    side = next(s for s in range(int(vecs**0.5), 0, -1) if vecs % s == 0)
    cores = 2 if rows % 2 == 0 else 1
    fine = Mesh(mesh.devices.reshape(rows // cores, cores, side, vecs // side), ("z", "core", "y", "x"))
    halves = [fine.shape[axis] == 2 for axis in ("core", "y", "x")]
    small = all(halves) and fine.shape["z"] & (fine.shape["z"] - 1) == 0
    row, vec = ("z", "core"), ("y", "x")

    def body(*args):
        return (fast if small else general)(*args)

    return jax.shard_map(
        body,
        mesh=fine,
        in_specs=(P(row, vec), P(None, row + vec, None), P(None, None, vec)),
        out_specs=P(row, vec),
        check_vma=False,
    )
```

```python
import functools

import jax
import jax.numpy as jnp
from jax import lax
from jax.experimental import pallas as pl
from jax.experimental.pallas import tpu as pltpu
from jax.sharding import Mesh, PartitionSpec as P


F32, BF16 = jnp.float32, jnp.bfloat16
NN = (((1,), (0,)), ((), ()))
NT = (((1,), (1,)), ((), ()))
PIECES = 8


def split(a):
    head = a.astype(BF16)
    return head, (a - head.astype(F32)).astype(BF16)


def dot3(a, b, dims):
    (ah, al), (bh, bl) = split(a), split(b)
    one = functools.partial(lax.dot_general, dimension_numbers=dims, preferred_element_type=F32)
    return one(ah, bh) + (one(ah, bl) + one(al, bh))


def place():
    return lax.axis_index("y") * 2 + lax.axis_index("x"), lax.axis_index("core")


def blocks_of(refs, skip=0):
    size = refs[0].shape[0]
    return [(i // 2, i % 2 * size, ref) for i, ref in enumerate(refs, skip)]


def window(v, block, first, size):
    return pl.ds(pl.multiple_of((v ^ block) * 2 * size + first, 8), size)


def project(current, refs, v, skip=0):
    total = None
    for block, first, ref in blocks_of(refs, skip):
        x = current[window(v, block, first, ref.shape[0]), :]
        part = dot3(x.T, ref[...], NN)
        total = part if total is None else total + part
    return total


def give_out(total, core, keep, send):
    half = keep.shape[0]
    mine = core == 0
    keep[...] = jnp.where(mine, total[:half], total[half:])
    send[...] = jnp.where(mine, total[half:], total[:half])


def early_kernel(x, *refs):
    v, _ = place()
    refs[-1][...] = project(x, refs[:-1], v)


def late_kernel(x, total, *refs):
    v, core = place()
    refs, (keep, send) = refs[:-2], refs[-2:]
    give_out(total[...] + project(x, refs, v, PIECES - len(refs)), core, keep, send)


def both_halves(mine, other, core):
    a, b = mine[...], other[...]
    first = core == 0
    return jnp.concatenate([jnp.where(first, a, b), jnp.where(first, b, a)], axis=0)


def update(current, out, refs, coefficients, v):
    for block, first, ref in blocks_of(refs):
        at = window(v, block, first, ref.shape[0])
        out[at, :] = current[at, :] - dot3(ref[...], coefficients, NT)


def turn_kernel(x, mine, other, *refs):
    v, core = place()
    old, new, (out, total) = refs[:PIECES], refs[PIECES:-2], refs[-2:]
    update(x, out, old, both_halves(mine, other, core), v)
    total[...] = project(out, new, v)


def last_kernel(x, mine, other, *refs):
    v, core = place()
    update(x, refs[PIECES], refs[:PIECES], both_halves(mine, other, core), v)


def solve_kernel(panel, n, *refs):
    v, core = place()
    total = refs[0][...]
    for i in range(1, n):
        total = total + refs[i][...]
    factor, first, across, exchanged, out = refs[n:]
    share = factor.shape[-1]
    on_x = core == 0
    own, along_x, along_y, far = split_columns(total, v, share)
    second = jnp.concatenate([exchanged[:, :share], exchanged[:, share : 2 * share]], axis=0)
    a, b = across[...], exchanged[:, 2 * share :]
    across = jnp.concatenate([jnp.where(on_x, a, b), jnp.where(on_x, b, a)], axis=0)
    sums = dot3(own, factor[panel], NT)
    sums += dot3(jnp.where(on_x, along_x, along_y), first[...], NT)
    sums += dot3(jnp.where(on_x, along_y, along_x), second, NT)
    out[...] = sums + dot3(far, across, NT)


def split_columns(total, v, share):
    b = [total[:, i * share : (i + 1) * share] for i in range(4)]
    odd, up = (v & 1) == 1, (v & 2) == 2
    p, q = jnp.where(odd, b[1], b[0]), jnp.where(odd, b[0], b[1])
    r, s = jnp.where(odd, b[3], b[2]), jnp.where(odd, b[2], b[3])
    return [jnp.where(up, r, p), jnp.where(up, s, q), jnp.where(up, p, r), jnp.where(up, q, s)]


def vmem(n):
    return [pl.BlockSpec(memory_space=pltpu.VMEM)] * n


def call(kernel, outs, args, flops):
    nbytes = sum(4 * a.size for a in args) + sum(4 * o.size for o in outs)
    return pl.pallas_call(
        kernel,
        out_shape=outs,
        in_specs=vmem(len(args)),
        out_specs=vmem(len(outs)),
        compiler_params=pltpu.CompilerParams(vmem_limit_bytes=12 * 2**20),
        cost_estimate=pl.CostEstimate(flops=flops, bytes_accessed=nbytes, transcendentals=0),
    )(*args)


def swap(a, axis, by=1):
    n = lax.axis_size(axis)
    return lax.ppermute(a, axis, [(i, i ^ by) for i in range(n)])


def gather(block):
    half = block.shape[0] // 2
    a, b = block[:half], block[half:]
    ya, xb = swap(a, "y"), swap(b, "x")
    xa, yb = swap(a, "x"), swap(b, "y")
    return a, b, xa, xb, ya, yb, swap(ya, "x"), swap(xb, "y")


def gather_factor(own):
    half, core = own.shape[0] // 2, lax.axis_index("core")
    axes = ("core", "y", "x")
    n = lax.axis_size(axes)
    first = lax.ppermute(own, axes, [(i, i ^ (2 if i >= n // 2 else 1)) for i in range(n)])
    mine = lax.dynamic_slice(own, (core * half, 0), (half, own.shape[1]))
    across = lax.ppermute(mine, axes, [(i, i ^ 3) for i in range(n)])
    joined = jnp.concatenate([first[:half], first[half:], across], axis=1)
    return first, across, swap(joined, "core")


def fast(vectors, reflectors, triangles):
    rows, share = vectors.shape
    panels, _, width = reflectors.shape
    sums = lax.axis_size("z")
    part = jax.ShapeDtypeStruct((share // 2, width), F32)
    whole = jax.ShapeDtypeStruct((rows, share), F32)
    work = 2 * rows * width * share
    top = panels - 1

    sections, factors = {}, {}
    for k in reversed(range(panels)):
        sections[k] = gather(reflectors[k])
        factors[k] = gather_factor(triangles[k])
        if k == top:
            pieces = list(sections[k])
            pieces[4], reflectors, triangles = lax.optimization_barrier((pieces[4], reflectors, triangles))
            sections[k] = tuple(pieces)

    def reduced(keep, send, k):
        s = keep + swap(send, "core")
        r = [swap(s, "z", by) for by in range(1, sums)]
        mine = call(
            functools.partial(solve_kernel, k, sums), [part], [s, *r, triangles, *factors[k]], width * width * share
        )[0]
        return mine, swap(mine, "core")

    total = jax.ShapeDtypeStruct((share, width), F32)
    ahead = {k: a[:-2] for k, a in sections.items()}
    sum_so_far = call(early_kernel, [total], [vectors, *ahead[top]], work * 3 // 4)[0]
    current = vectors
    for k in reversed(range(panels)):
        keep, send = call(late_kernel, [part, part], [current, sum_so_far, *sections[k][-2:]], work // 4)
        c = reduced(keep, send, k)
        if k > 0:
            current, sum_so_far = call(
                turn_kernel, [whole, total], [current, *c, *sections[k], *ahead[k - 1]], work * 7 // 4
            )
    return call(last_kernel, [whole], [current, *c, *sections[0]], work)[0]


def general(vectors, reflectors, triangles):
    highest = lax.Precision.HIGHEST
    row, vec = ("z", "core"), ("y", "x")
    current = vectors
    for panel in reversed(range(reflectors.shape[0])):
        section = lax.all_gather(reflectors[panel], vec, axis=0, tiled=True)
        factor = lax.all_gather(triangles[panel], vec, axis=1, tiled=True)
        partial_value = lax.dot_general(
            section, current, (((0,), (0,)), ((), ())), precision=highest, preferred_element_type=F32
        )
        share = lax.psum_scatter(partial_value, row, scatter_dimension=1, tiled=True)
        owned = jnp.dot(factor, share, precision=highest, preferred_element_type=F32)
        coefficients = lax.all_gather(owned, row, axis=1, tiled=True)
        current = current - jnp.dot(section, coefficients, precision=highest, preferred_element_type=F32)
    return current


def solution(mesh):
    rows, vecs = mesh.shape["row"], mesh.shape["vec"]
    side = next(s for s in range(int(vecs**0.5), 0, -1) if vecs % s == 0)
    cores = 2 if rows % 2 == 0 else 1
    fine = Mesh(mesh.devices.reshape(rows // cores, cores, side, vecs // side), ("z", "core", "y", "x"))
    halves = [fine.shape[axis] == 2 for axis in ("core", "y", "x")]
    small = all(halves) and fine.shape["z"] & (fine.shape["z"] - 1) == 0
    row, vec = ("z", "core"), ("y", "x")

    def body(*args):
        return (fast if small else general)(*args)

    return jax.shard_map(
        body,
        mesh=fine,
        in_specs=(P(row, vec), P(None, row + vec, None), P(None, None, vec)),
        out_specs=P(row, vec),
        check_vma=False,
    )
```

```python
import functools

import jax
import jax.numpy as jnp
from jax import lax
from jax.experimental import pallas as pl
from jax.experimental.pallas import tpu as pltpu
from jax.sharding import Mesh, PartitionSpec as P


F32, BF16 = jnp.float32, jnp.bfloat16
NN = (((1,), (0,)), ((), ()))
NT = (((1,), (1,)), ((), ()))
PIECES = 8


def split(a):
    head = a.astype(BF16)
    return head, (a - head.astype(F32)).astype(BF16)


def dot3(a, b, dims):
    (ah, al), (bh, bl) = split(a), split(b)
    one = functools.partial(lax.dot_general, dimension_numbers=dims, preferred_element_type=F32)
    return one(ah, bh) + (one(ah, bl) + one(al, bh))


def place():
    return lax.axis_index("y") * 2 + lax.axis_index("x"), lax.axis_index("core")


def blocks_of(refs, skip=0):
    size = refs[0].shape[0]
    return [(i // 2, i % 2 * size, ref) for i, ref in enumerate(refs, skip)]


def window(v, block, first, size):
    return pl.ds(pl.multiple_of((v ^ block) * 2 * size + first, 8), size)


def project(current, refs, v, skip=0):
    total = None
    for block, first, ref in blocks_of(refs, skip):
        x = current[window(v, block, first, ref.shape[0]), :]
        part = dot3(x.T, ref[...], NN)
        total = part if total is None else total + part
    return total


def give_out(total, core, keep, send):
    half = keep.shape[0]
    mine = core == 0
    keep[...] = jnp.where(mine, total[:half], total[half:])
    send[...] = jnp.where(mine, total[half:], total[:half])


def early_kernel(x, *refs):
    v, _ = place()
    refs[-1][...] = project(x, refs[:-1], v)


def late_kernel(x, total, *refs):
    v, core = place()
    refs, (keep, send) = refs[:-2], refs[-2:]
    give_out(total[...] + project(x, refs, v, PIECES - len(refs)), core, keep, send)


def both_halves(mine, other, core):
    a, b = mine[...], other[...]
    first = core == 0
    return jnp.concatenate([jnp.where(first, a, b), jnp.where(first, b, a)], axis=0)


def update(current, out, refs, coefficients, v):
    for block, first, ref in blocks_of(refs):
        at = window(v, block, first, ref.shape[0])
        out[at, :] = current[at, :] - dot3(ref[...], coefficients, NT)


def turn_kernel(x, mine, other, *refs):
    v, core = place()
    old, new, (out, total) = refs[:PIECES], refs[PIECES:-2], refs[-2:]
    update(x, out, old, both_halves(mine, other, core), v)
    total[...] = project(out, new, v)


def last_kernel(x, mine, other, *refs):
    v, core = place()
    update(x, refs[PIECES], refs[:PIECES], both_halves(mine, other, core), v)


def cut_kernel(x, out):
    half = out.shape[0]
    out[...] = jnp.where(lax.axis_index("core") == 0, x[:half], x[half:])


def join_kernel(first, across, out):
    half, share = across.shape
    out[:, :share] = first[:half]
    out[:, share : 2 * share] = first[half:]
    out[:, 2 * share :] = across[...]


def hold_kernel(x, out):
    out[...] = x[...]


def solve_kernel(panel, n, *refs):
    v, core = place()
    total = refs[0][...]
    for i in range(1, n):
        total = total + refs[i][...]
    factor, first, across, exchanged, out = refs[n:]
    share = factor.shape[-1]
    on_x = core == 0
    own, along_x, along_y, far = split_columns(total, v, share)
    second = jnp.concatenate([exchanged[:, :share], exchanged[:, share : 2 * share]], axis=0)
    a, b = across[...], exchanged[:, 2 * share :]
    across = jnp.concatenate([jnp.where(on_x, a, b), jnp.where(on_x, b, a)], axis=0)
    sums = dot3(own, factor[panel], NT)
    sums += dot3(jnp.where(on_x, along_x, along_y), first[...], NT)
    sums += dot3(jnp.where(on_x, along_y, along_x), second, NT)
    out[...] = sums + dot3(far, across, NT)


def split_columns(total, v, share):
    b = [total[:, i * share : (i + 1) * share] for i in range(4)]
    odd, up = (v & 1) == 1, (v & 2) == 2
    p, q = jnp.where(odd, b[1], b[0]), jnp.where(odd, b[0], b[1])
    r, s = jnp.where(odd, b[3], b[2]), jnp.where(odd, b[2], b[3])
    return [jnp.where(up, r, p), jnp.where(up, s, q), jnp.where(up, p, r), jnp.where(up, q, s)]


def vmem(n):
    return [pl.BlockSpec(memory_space=pltpu.VMEM)] * n


def call(kernel, outs, args, flops):
    nbytes = sum(4 * a.size for a in args) + sum(4 * o.size for o in outs)
    return pl.pallas_call(
        kernel,
        out_shape=outs,
        in_specs=vmem(len(args)),
        out_specs=vmem(len(outs)),
        compiler_params=pltpu.CompilerParams(vmem_limit_bytes=8 * 2**20),
        cost_estimate=pl.CostEstimate(flops=flops, bytes_accessed=nbytes, transcendentals=0),
    )(*args)


def swap(a, axis, by=1):
    n = lax.axis_size(axis)
    return lax.ppermute(a, axis, [(i, i ^ by) for i in range(n)])


def gather(block):
    half = block.shape[0] // 2
    a, b = block[:half], block[half:]
    ya, xb = swap(a, "y"), swap(b, "x")
    xa, yb = swap(a, "x"), swap(b, "y")
    return a, b, xa, xb, ya, yb, swap(ya, "x"), swap(xb, "y")


def gather_factor(own):
    half, share = own.shape[0] // 2, own.shape[1]
    axes = ("core", "y", "x")
    n = lax.axis_size(axes)
    first = lax.ppermute(own, axes, [(i, i ^ (2 if i >= n // 2 else 1)) for i in range(n)])
    mine = call(cut_kernel, [jax.ShapeDtypeStruct((half, share), F32)], [first], 0)[0]
    across = lax.ppermute(mine, axes, [(i, i ^ (1 if i >= n // 2 else 2)) for i in range(n)])
    joined = call(join_kernel, [jax.ShapeDtypeStruct((half, 3 * share), F32)], [first, across], 0)[0]
    return first, across, swap(joined, "core")


def fast(vectors, reflectors, triangles):
    rows, share = vectors.shape
    panels, _, width = reflectors.shape
    sums = lax.axis_size("z")
    part = jax.ShapeDtypeStruct((share // 2, width), F32)
    whole = jax.ShapeDtypeStruct((rows, share), F32)
    work = 2 * rows * width * share
    top = panels - 1

    sections, factors = {}, {}
    for k in reversed(range(panels)):
        sections[k] = gather(reflectors[k])
        factors[k] = gather_factor(triangles[k])
        if k == top:
            pieces = list(sections[k])
            pieces[4], reflectors, triangles = lax.optimization_barrier((pieces[4], reflectors, triangles))
            sections[k] = tuple(pieces)

    def reduced(keep, send, k):
        s = keep + swap(send, "core")
        r = [swap(s, "z", by) for by in range(1, sums)]
        s = call(hold_kernel, [part], [s], 0)[0]
        mine = call(
            functools.partial(solve_kernel, k, sums), [part], [s, *r, triangles, *factors[k]], width * width * share
        )[0]
        return mine, swap(mine, "core")

    total = jax.ShapeDtypeStruct((share, width), F32)
    ahead = {k: a[:-2] for k, a in sections.items()}
    sum_so_far = call(early_kernel, [total], [vectors, *ahead[top]], work * 3 // 4)[0]
    current = vectors
    for k in reversed(range(panels)):
        keep, send = call(late_kernel, [part, part], [current, sum_so_far, *sections[k][-2:]], work // 4)
        c = reduced(keep, send, k)
        if k > 0:
            current, sum_so_far = call(
                turn_kernel, [whole, total], [current, *c, *sections[k], *ahead[k - 1]], work * 7 // 4
            )
    return call(last_kernel, [whole], [current, *c, *sections[0]], work)[0]


def general(vectors, reflectors, triangles):
    highest = lax.Precision.HIGHEST
    row, vec = ("z", "core"), ("y", "x")
    current = vectors
    for panel in reversed(range(reflectors.shape[0])):
        section = lax.all_gather(reflectors[panel], vec, axis=0, tiled=True)
        factor = lax.all_gather(triangles[panel], vec, axis=1, tiled=True)
        partial_value = lax.dot_general(
            section, current, (((0,), (0,)), ((), ())), precision=highest, preferred_element_type=F32
        )
        share = lax.psum_scatter(partial_value, row, scatter_dimension=1, tiled=True)
        owned = jnp.dot(factor, share, precision=highest, preferred_element_type=F32)
        coefficients = lax.all_gather(owned, row, axis=1, tiled=True)
        current = current - jnp.dot(section, coefficients, precision=highest, preferred_element_type=F32)
    return current


def solution(mesh):
    rows, vecs = mesh.shape["row"], mesh.shape["vec"]
    side = next(s for s in range(int(vecs**0.5), 0, -1) if vecs % s == 0)
    cores = 2 if rows % 2 == 0 else 1
    fine = Mesh(mesh.devices.reshape(rows // cores, cores, side, vecs // side), ("z", "core", "y", "x"))
    halves = [fine.shape[axis] == 2 for axis in ("core", "y", "x")]
    small = all(halves) and fine.shape["z"] & (fine.shape["z"] - 1) == 0
    row, vec = ("z", "core"), ("y", "x")

    def body(*args):
        return (fast if small else general)(*args)

    return jax.shard_map(
        body,
        mesh=fine,
        in_specs=(P(row, vec), P(None, row + vec, None), P(None, None, vec)),
        out_specs=P(row, vec),
        check_vma=False,
    )
```

```python
import functools

import jax
import jax.numpy as jnp
from jax import lax
from jax.experimental import pallas as pl
from jax.experimental.pallas import tpu as pltpu
from jax.sharding import Mesh, PartitionSpec as P


F32, BF16 = jnp.float32, jnp.bfloat16
NN = (((1,), (0,)), ((), ()))
NT = (((1,), (1,)), ((), ()))
PIECES = 8


def split(a):
    head = a.astype(BF16)
    return head, (a - head.astype(F32)).astype(BF16)


def dot(a, b, dims):
    return lax.dot_general(a, b, dims, preferred_element_type=F32)


def stack(pair):
    return jnp.concatenate(pair, axis=0)


def dot_left(a, b, dims):
    ah, al = split(a)
    bh, bl = split(b)
    n = a.shape[0]
    both = dot(stack((ah, al)), bh, dims)
    return both[:n] + (both[n:] + dot(ah, bl, dims))


def dot_right(a, stacked, dims):
    ah, al = split(a)
    n = stacked.shape[0] // 2
    both = dot(ah, stacked, dims)
    return both[:, :n] + (both[:, n:] + dot(al, stacked[:n], dims))


def place():
    return lax.axis_index("y") * 2 + lax.axis_index("x"), lax.axis_index("core")


def blocks_of(refs, skip=0):
    size = refs[0].shape[0]
    return [(i // 2, i % 2 * size, ref) for i, ref in enumerate(refs, skip)]


def window(v, block, first, size):
    return pl.ds(pl.multiple_of((v ^ block) * 2 * size + first, 8), size)


def project(current, refs, v, skip=0):
    total = None
    for block, first, ref in blocks_of(refs, skip):
        x = current[window(v, block, first, ref.shape[0]), :]
        part = dot_left(x.T, ref[...], NN)
        total = part if total is None else total + part
    return total


def give_out(total, core, keep, send):
    half = keep.shape[0]
    mine = core == 0
    keep[...] = jnp.where(mine, total[:half], total[half:])
    send[...] = jnp.where(mine, total[half:], total[:half])


def early_kernel(x, *refs):
    v, _ = place()
    refs[-1][...] = project(x, refs[:-1], v)


def late_kernel(x, total, *refs):
    v, core = place()
    refs, (keep, send) = refs[:-2], refs[-2:]
    give_out(total[...] + project(x, refs, v, PIECES - len(refs)), core, keep, send)


def both_halves(mine, other, core):
    a, b = mine[...], other[...]
    first = core == 0
    return jnp.concatenate([jnp.where(first, a, b), jnp.where(first, b, a)], axis=0)


def update(current, out, refs, coefficients, v):
    stacked = stack(split(coefficients))
    for block, first, ref in blocks_of(refs):
        at = window(v, block, first, ref.shape[0])
        out[at, :] = current[at, :] - dot_right(ref[...], stacked, NT)


def turn_kernel(x, mine, other, *refs):
    v, core = place()
    old, new, (out, total) = refs[:PIECES], refs[PIECES:-2], refs[-2:]
    update(x, out, old, both_halves(mine, other, core), v)
    total[...] = project(out, new, v)


def last_kernel(x, mine, other, *refs):
    v, core = place()
    update(x, refs[PIECES], refs[:PIECES], both_halves(mine, other, core), v)


def cut_kernel(x, out):
    half = out.shape[0]
    out[...] = jnp.where(lax.axis_index("core") == 0, x[:half], x[half:])


def join_kernel(first, across, out):
    half, share = across.shape
    out[:, :share] = first[:half]
    out[:, share : 2 * share] = first[half:]
    out[:, 2 * share :] = across[...]


def hold_kernel(x, out):
    out[...] = x[...]


def solve_kernel(panel, n, *refs):
    v, core = place()
    total = refs[0][...]
    for i in range(1, n):
        total = total + refs[i][...]
    factor, first, across, exchanged, out = refs[n:]
    share = factor.shape[-1]
    on_x = core == 0
    own, along_x, along_y, far = split_columns(total, v, share)
    second = jnp.concatenate([exchanged[:, :share], exchanged[:, share : 2 * share]], axis=0)
    a, b = across[...], exchanged[:, 2 * share :]
    across = jnp.concatenate([jnp.where(on_x, a, b), jnp.where(on_x, b, a)], axis=0)
    sums = dot_left(own, factor[panel], NT)
    sums += dot_left(jnp.where(on_x, along_x, along_y), first[...], NT)
    sums += dot_left(jnp.where(on_x, along_y, along_x), second, NT)
    out[...] = sums + dot_left(far, across, NT)


def split_columns(total, v, share):
    b = [total[:, i * share : (i + 1) * share] for i in range(4)]
    odd, up = (v & 1) == 1, (v & 2) == 2
    p, q = jnp.where(odd, b[1], b[0]), jnp.where(odd, b[0], b[1])
    r, s = jnp.where(odd, b[3], b[2]), jnp.where(odd, b[2], b[3])
    return [jnp.where(up, r, p), jnp.where(up, s, q), jnp.where(up, p, r), jnp.where(up, q, s)]


def vmem(n):
    return [pl.BlockSpec(memory_space=pltpu.VMEM)] * n


def call(kernel, outs, args, flops):
    nbytes = sum(4 * a.size for a in args) + sum(4 * o.size for o in outs)
    return pl.pallas_call(
        kernel,
        out_shape=outs,
        in_specs=vmem(len(args)),
        out_specs=vmem(len(outs)),
        compiler_params=pltpu.CompilerParams(vmem_limit_bytes=8 * 2**20),
        cost_estimate=pl.CostEstimate(flops=flops, bytes_accessed=nbytes, transcendentals=0),
    )(*args)


def swap(a, axis, by=1):
    n = lax.axis_size(axis)
    return lax.ppermute(a, axis, [(i, i ^ by) for i in range(n)])


def gather(block):
    half = block.shape[0] // 2
    a, b = block[:half], block[half:]
    ya, xb = swap(a, "y"), swap(b, "x")
    xa, yb = swap(a, "x"), swap(b, "y")
    return a, b, xa, xb, ya, yb, swap(ya, "x"), swap(xb, "y")


def gather_factor(own):
    half, share = own.shape[0] // 2, own.shape[1]
    axes = ("core", "y", "x")
    n = lax.axis_size(axes)
    first = lax.ppermute(own, axes, [(i, i ^ (2 if i >= n // 2 else 1)) for i in range(n)])
    mine = call(cut_kernel, [jax.ShapeDtypeStruct((half, share), F32)], [first], 0)[0]
    across = lax.ppermute(mine, axes, [(i, i ^ (1 if i >= n // 2 else 2)) for i in range(n)])
    joined = call(join_kernel, [jax.ShapeDtypeStruct((half, 3 * share), F32)], [first, across], 0)[0]
    return first, across, swap(joined, "core")


def fast(vectors, reflectors, triangles):
    rows, share = vectors.shape
    panels, _, width = reflectors.shape
    sums = lax.axis_size("z")
    part = jax.ShapeDtypeStruct((share // 2, width), F32)
    whole = jax.ShapeDtypeStruct((rows, share), F32)
    work = 2 * rows * width * share
    top = panels - 1

    sections, factors = {}, {}
    for k in reversed(range(panels)):
        sections[k] = gather(reflectors[k])
        factors[k] = gather_factor(triangles[k])
        if k == top:
            pieces = list(sections[k])
            pieces[4], reflectors, triangles = lax.optimization_barrier((pieces[4], reflectors, triangles))
            sections[k] = tuple(pieces)

    def reduced(keep, send, k):
        s = keep + swap(send, "core")
        r = [swap(s, "z", by) for by in range(1, sums)]
        s = call(hold_kernel, [part], [s], 0)[0]
        mine = call(
            functools.partial(solve_kernel, k, sums), [part], [s, *r, triangles, *factors[k]], width * width * share
        )[0]
        return mine, swap(mine, "core")

    total = jax.ShapeDtypeStruct((share, width), F32)
    ahead = {k: a[:-2] for k, a in sections.items()}
    sum_so_far = call(early_kernel, [total], [vectors, *ahead[top]], work * 3 // 4)[0]
    current = vectors
    for k in reversed(range(panels)):
        keep, send = call(late_kernel, [part, part], [current, sum_so_far, *sections[k][-2:]], work // 4)
        c = reduced(keep, send, k)
        if k > 0:
            current, sum_so_far = call(
                turn_kernel, [whole, total], [current, *c, *sections[k], *ahead[k - 1]], work * 7 // 4
            )
    return call(last_kernel, [whole], [current, *c, *sections[0]], work)[0]


def general(vectors, reflectors, triangles):
    highest = lax.Precision.HIGHEST
    row, vec = ("z", "core"), ("y", "x")
    current = vectors
    for panel in reversed(range(reflectors.shape[0])):
        section = lax.all_gather(reflectors[panel], vec, axis=0, tiled=True)
        factor = lax.all_gather(triangles[panel], vec, axis=1, tiled=True)
        partial_value = lax.dot_general(
            section, current, (((0,), (0,)), ((), ())), precision=highest, preferred_element_type=F32
        )
        share = lax.psum_scatter(partial_value, row, scatter_dimension=1, tiled=True)
        owned = jnp.dot(factor, share, precision=highest, preferred_element_type=F32)
        coefficients = lax.all_gather(owned, row, axis=1, tiled=True)
        current = current - jnp.dot(section, coefficients, precision=highest, preferred_element_type=F32)
    return current


def solution(mesh):
    rows, vecs = mesh.shape["row"], mesh.shape["vec"]
    side = next(s for s in range(int(vecs**0.5), 0, -1) if vecs % s == 0)
    cores = 2 if rows % 2 == 0 else 1
    fine = Mesh(mesh.devices.reshape(rows // cores, cores, side, vecs // side), ("z", "core", "y", "x"))
    halves = [fine.shape[axis] == 2 for axis in ("core", "y", "x")]
    small = all(halves) and fine.shape["z"] & (fine.shape["z"] - 1) == 0
    row, vec = ("z", "core"), ("y", "x")

    def body(*args):
        return (fast if small else general)(*args)

    return jax.shard_map(
        body,
        mesh=fine,
        in_specs=(P(row, vec), P(None, row + vec, None), P(None, None, vec)),
        out_specs=P(row, vec),
        check_vma=False,
    )
```

```python
import functools

import jax
import jax.numpy as jnp
from jax import lax
from jax.experimental import pallas as pl
from jax.experimental.pallas import tpu as pltpu
from jax.sharding import Mesh, PartitionSpec as P


F32, BF16 = jnp.float32, jnp.bfloat16
NN = (((1,), (0,)), ((), ()))
NT = (((1,), (1,)), ((), ()))
PIECES = 8


def split(a):
    head = a.astype(BF16)
    return head, (a - head.astype(F32)).astype(BF16)


def dot(a, b, dims):
    return lax.dot_general(a, b, dims, preferred_element_type=F32)


def stack(pair):
    return jnp.concatenate(pair, axis=0)


def dot_left(a, b, dims):
    ah, al = split(a)
    bh, bl = split(b)
    n = a.shape[0]
    both = dot(stack((ah, al)), bh, dims)
    return both[:n] + (both[n:] + dot(ah, bl, dims))


def dot_right(a, b):
    ah, al = split(a)
    n = b.shape[1] // 2
    both = dot(ah, b, NN)
    return both[:, :n] + (both[:, n:] + dot(al, b[:, :n], NN))


def place():
    return lax.axis_index("y") * 2 + lax.axis_index("x"), lax.axis_index("core")


def blocks_of(refs, skip=0):
    size = refs[0].shape[0]
    return [(i // 2, i % 2 * size, ref) for i, ref in enumerate(refs, skip)]


def window(v, block, first, size):
    return pl.ds(pl.multiple_of((v ^ block) * 2 * size + first, 8), size)


def project(current, refs, v, skip=0):
    x, r = [], []
    for block, first, ref in blocks_of(refs, skip):
        x.append(current[window(v, block, first, ref.shape[0]), :].T)
        r.append(ref[...])
    return dot_left(jnp.concatenate(x, axis=1), jnp.concatenate(r, axis=0), NN)


def give_out(total, core, keep, send):
    half = keep.shape[0]
    mine = core == 0
    keep[...] = jnp.where(mine, total[:half], total[half:])
    send[...] = jnp.where(mine, total[half:], total[:half])


def early_kernel(x, *refs):
    v, _ = place()
    refs[-1][...] = project(x, refs[:-1], v)


def late_kernel(x, total, *refs):
    v, core = place()
    refs, (keep, send) = refs[:-2], refs[-2:]
    give_out(total[...] + project(x, refs, v, PIECES - len(refs)), core, keep, send)


def coefficients(mine, other, core):
    a, b = mine[...], other[...]
    first = core == 0
    rows = jnp.concatenate([jnp.where(first, a, b), jnp.where(first, b, a)], axis=0)
    return jnp.concatenate(split(rows.T), axis=1)


def update(current, out, refs, c, v, after=None):
    for i, (block, first, ref) in enumerate(blocks_of(refs)):
        at = window(v, block, first, ref.shape[0])
        out[at, :] = current[at, :] - dot_right(ref[...], c)
        if after is not None:
            after(i, at)


def turn_kernel(x, mine, other, *refs):
    v, core = place()
    old, new, (out, total) = refs[:PIECES], refs[PIECES:-2], refs[-2:]
    update(x, out, old, coefficients(mine, other, core), v)
    total[...] = project(out, new, v)


def last_kernel(x, mine, other, *refs):
    v, core = place()
    refs, (out, made, sems) = refs[:PIECES], refs[PIECES:]
    copies = []

    def leave(i, at):
        copies.append(pltpu.make_async_copy(made.at[at, :], out.at[at, :], sems.at[i]))
        copies[-1].start()

    update(x, made, refs, coefficients(mine, other, core), v, leave)
    for copy in copies:
        copy.wait()


def cut_kernel(x, out):
    half = out.shape[0]
    out[...] = jnp.where(lax.axis_index("core") == 0, x[:half], x[half:])


def join_kernel(first, across, out):
    half, share = across.shape
    out[:, :share] = first[:half]
    out[:, share : 2 * share] = first[half:]
    out[:, 2 * share :] = across[...]


def hold_kernel(x, out):
    out[...] = x[...]


def solve_kernel(panel, n, *refs):
    v, core = place()
    total = refs[0][...]
    for i in range(1, n):
        total = total + refs[i][...]
    factor, first, across, exchanged, out = refs[n:]
    share = factor.shape[-1]
    on_x = core == 0
    own, along_x, along_y, far = split_columns(total, v, share)
    second = jnp.concatenate([exchanged[:, :share], exchanged[:, share : 2 * share]], axis=0)
    a, b = across[...], exchanged[:, 2 * share :]
    across = jnp.concatenate([jnp.where(on_x, a, b), jnp.where(on_x, b, a)], axis=0)
    sums = dot_left(own, factor[panel], NT)
    sums += dot_left(jnp.where(on_x, along_x, along_y), first[...], NT)
    sums += dot_left(jnp.where(on_x, along_y, along_x), second, NT)
    out[...] = sums + dot_left(far, across, NT)


def split_columns(total, v, share):
    b = [total[:, i * share : (i + 1) * share] for i in range(4)]
    odd, up = (v & 1) == 1, (v & 2) == 2
    p, q = jnp.where(odd, b[1], b[0]), jnp.where(odd, b[0], b[1])
    r, s = jnp.where(odd, b[3], b[2]), jnp.where(odd, b[2], b[3])
    return [jnp.where(up, r, p), jnp.where(up, s, q), jnp.where(up, p, r), jnp.where(up, q, s)]


def vmem(n):
    return [pl.BlockSpec(memory_space=pltpu.VMEM)] * n


def call(kernel, outs, args, flops, out_space=pltpu.VMEM, scratch=()):
    nbytes = sum(4 * a.size for a in args) + sum(4 * o.size for o in outs)
    return pl.pallas_call(
        kernel,
        out_shape=outs,
        in_specs=vmem(len(args)),
        out_specs=[pl.BlockSpec(memory_space=out_space)] * len(outs),
        scratch_shapes=list(scratch),
        compiler_params=pltpu.CompilerParams(vmem_limit_bytes=8 * 2**20),
        cost_estimate=pl.CostEstimate(flops=flops, bytes_accessed=nbytes, transcendentals=0),
    )(*args)


def swap(a, axis, by=1):
    n = lax.axis_size(axis)
    return lax.ppermute(a, axis, [(i, i ^ by) for i in range(n)])


def gather(block, first):
    half = block.shape[0] // 2
    a = block[:half]
    if first:
        a, block = lax.optimization_barrier((a, block))
    b = block[half:]
    ya, xb = swap(a, "y"), swap(b, "x")
    xa, yb = swap(a, "x"), swap(b, "y")
    return a, b, xa, xb, ya, yb, swap(ya, "x"), swap(xb, "y")


def gather_factor(own):
    half, share = own.shape[0] // 2, own.shape[1]
    axes = ("core", "y", "x")
    n = lax.axis_size(axes)
    first = lax.ppermute(own, axes, [(i, i ^ (2 if i >= n // 2 else 1)) for i in range(n)])
    mine = call(cut_kernel, [jax.ShapeDtypeStruct((half, share), F32)], [first], 0)[0]
    across = lax.ppermute(mine, axes, [(i, i ^ (1 if i >= n // 2 else 2)) for i in range(n)])
    joined = call(join_kernel, [jax.ShapeDtypeStruct((half, 3 * share), F32)], [first, across], 0)[0]
    return first, across, swap(joined, "core")


def fast(vectors, reflectors, triangles):
    rows, share = vectors.shape
    panels, _, width = reflectors.shape
    sums = lax.axis_size("z")
    part = jax.ShapeDtypeStruct((share // 2, width), F32)
    whole = jax.ShapeDtypeStruct((rows, share), F32)
    work = 2 * rows * width * share
    top = panels - 1

    sections, factors = {}, {}
    for k in reversed(range(panels)):
        sections[k] = gather(reflectors[k], k == top)
        factors[k] = gather_factor(triangles[k])
        if k == top:
            pieces = list(sections[k])
            pieces[4], reflectors, triangles = lax.optimization_barrier((pieces[4], reflectors, triangles))
            sections[k] = tuple(pieces)

    def reduced(keep, send, k):
        s = keep + swap(send, "core")
        r = [swap(s, "z", by) for by in range(1, sums)]
        s = call(hold_kernel, [part], [s], 0)[0]
        mine = call(
            functools.partial(solve_kernel, k, sums), [part], [s, *r, triangles, *factors[k]], width * width * share
        )[0]
        return mine, swap(mine, "core")

    total = jax.ShapeDtypeStruct((share, width), F32)
    ahead = {k: a[:-2] for k, a in sections.items()}
    sum_so_far = call(early_kernel, [total], [vectors, *ahead[top]], work * 3 // 4)[0]
    current = vectors
    for k in reversed(range(panels)):
        keep, send = call(late_kernel, [part, part], [current, sum_so_far, *sections[k][-2:]], work // 4)
        c = reduced(keep, send, k)
        if k > 0:
            current, sum_so_far = call(
                turn_kernel, [whole, total], [current, *c, *sections[k], *ahead[k - 1]], work * 7 // 4
            )
    scratch = [pltpu.VMEM(whole.shape, F32), pltpu.SemaphoreType.DMA((PIECES,))]
    return call(last_kernel, [whole], [current, *c, *sections[0]], work, pl.ANY, scratch)[0]


def general(vectors, reflectors, triangles):
    highest = lax.Precision.HIGHEST
    row, vec = ("z", "core"), ("y", "x")
    current = vectors
    for panel in reversed(range(reflectors.shape[0])):
        section = lax.all_gather(reflectors[panel], vec, axis=0, tiled=True)
        factor = lax.all_gather(triangles[panel], vec, axis=1, tiled=True)
        partial_value = lax.dot_general(
            section, current, (((0,), (0,)), ((), ())), precision=highest, preferred_element_type=F32
        )
        share = lax.psum_scatter(partial_value, row, scatter_dimension=1, tiled=True)
        owned = jnp.dot(factor, share, precision=highest, preferred_element_type=F32)
        coefficients = lax.all_gather(owned, row, axis=1, tiled=True)
        current = current - jnp.dot(section, coefficients, precision=highest, preferred_element_type=F32)
    return current


def solution(mesh):
    rows, vecs = mesh.shape["row"], mesh.shape["vec"]
    side = next(s for s in range(int(vecs**0.5), 0, -1) if vecs % s == 0)
    cores = 2 if rows % 2 == 0 else 1
    fine = Mesh(mesh.devices.reshape(rows // cores, cores, side, vecs // side), ("z", "core", "y", "x"))
    halves = [fine.shape[axis] == 2 for axis in ("core", "y", "x")]
    small = all(halves) and fine.shape["z"] & (fine.shape["z"] - 1) == 0
    row, vec = ("z", "core"), ("y", "x")

    def body(*args):
        return (fast if small else general)(*args)

    return jax.shard_map(
        body,
        mesh=fine,
        in_specs=(P(row, vec), P(None, row + vec, None), P(None, None, vec)),
        out_specs=P(row, vec),
        check_vma=False,
    )
```

```python
import functools

import jax
import jax.numpy as jnp
from jax import lax
from jax.experimental import pallas as pl
from jax.experimental.pallas import tpu as pltpu
from jax.sharding import Mesh, PartitionSpec as P


F32, BF16 = jnp.float32, jnp.bfloat16
NN = (((1,), (0,)), ((), ()))
NT = (((1,), (1,)), ((), ()))
PIECES = 8


def split(a):
    head = a.astype(BF16)
    return head, (a - head.astype(F32)).astype(BF16)


def dot(a, b, dims):
    return lax.dot_general(a, b, dims, preferred_element_type=F32)


def stack(pair):
    return jnp.concatenate(pair, axis=0)


def dot_left(a, b, dims):
    ah, al = split(a)
    bh, bl = split(b)
    n = a.shape[0]
    both = dot(stack((ah, al)), bh, dims)
    return both[:n] + (both[n:] + dot(ah, bl, dims))


def dot_right(a, b):
    ah, al = split(a)
    n = b.shape[1] // 2
    both = dot(ah, b, NN)
    return both[:, :n] + (both[:, n:] + dot(al, b[:, :n], NN))


def place():
    return lax.axis_index("y") * 2 + lax.axis_index("x"), lax.axis_index("core")


def blocks_of(refs, skip=0):
    size = refs[0].shape[0]
    return [(i // 2, i % 2 * size, ref) for i, ref in enumerate(refs, skip)]


def window(v, block, first, size):
    return pl.ds(pl.multiple_of((v ^ block) * 2 * size + first, 8), size)


def project(current, refs, v, skip=0):
    x, r = [], []
    for block, first, ref in blocks_of(refs, skip):
        x.append(current[window(v, block, first, ref.shape[0]), :].T)
        r.append(ref[...])
    return dot_left(jnp.concatenate(x, axis=1), jnp.concatenate(r, axis=0), NN)


def give_out(total, core, keep, send):
    half = keep.shape[0]
    mine = core == 0
    keep[...] = jnp.where(mine, total[:half], total[half:])
    send[...] = jnp.where(mine, total[half:], total[:half])


def early_kernel(x, *refs):
    v, _ = place()
    refs[-1][...] = project(x, refs[:-1], v)


def late_kernel(x, total, *refs):
    v, core = place()
    refs, (keep, send) = refs[:-2], refs[-2:]
    give_out(total[...] + project(x, refs, v, PIECES - len(refs)), core, keep, send)


def coefficients(mine, other, core):
    a, b = mine[...], other[...]
    first = core == 0
    rows = jnp.concatenate([jnp.where(first, a, b), jnp.where(first, b, a)], axis=0)
    return jnp.concatenate(split(rows.T), axis=1)


def update(current, out, refs, c, v, after=None):
    for i, (block, first, ref) in enumerate(blocks_of(refs)):
        at = window(v, block, first, ref.shape[0])
        out[at, :] = current[at, :] - dot_right(ref[...], c)
        if after is not None:
            after(i, at)


def turn_kernel(x, mine, other, *refs):
    v, core = place()
    old, new, (out, total) = refs[:PIECES], refs[PIECES:-2], refs[-2:]
    update(x, out, old, coefficients(mine, other, core), v)
    total[...] = project(out, new, v)


def last_kernel(x, mine, other, *refs):
    v, core = place()
    refs, (out, made, sems) = refs[:PIECES], refs[PIECES:]
    copies = []

    def leave(i, at):
        copies.append(pltpu.make_async_copy(made.at[at, :], out.at[at, :], sems.at[i]))
        copies[-1].start()

    update(x, made, refs, coefficients(mine, other, core), v, leave)
    for copy in copies:
        copy.wait()


def cut_kernel(x, out):
    half = out.shape[0]
    out[...] = jnp.where(lax.axis_index("core") == 0, x[:half], x[half:])


def join_kernel(first, across, out):
    half, share = across.shape
    out[:, :share] = first[:half]
    out[:, share : 2 * share] = first[half:]
    out[:, 2 * share :] = across[...]


def hold_kernel(x, out):
    out[...] = x[...]


def solve_kernel(panel, n, *refs):
    v, core = place()
    total = refs[0][...]
    for i in range(1, n):
        total = total + refs[i][...]
    factor, first, across, exchanged, out = refs[n:]
    share = factor.shape[-1]
    on_x = core == 0
    own, along_x, along_y, far = split_columns(total, v, share)
    second = jnp.concatenate([exchanged[:, :share], exchanged[:, share : 2 * share]], axis=0)
    a, b = across[...], exchanged[:, 2 * share :]
    across = jnp.concatenate([jnp.where(on_x, a, b), jnp.where(on_x, b, a)], axis=0)
    sums = dot_left(own, factor[panel], NT)
    sums += dot_left(jnp.where(on_x, along_x, along_y), first[...], NT)
    sums += dot_left(jnp.where(on_x, along_y, along_x), second, NT)
    out[...] = sums + dot_left(far, across, NT)


def split_columns(total, v, share):
    b = [total[:, i * share : (i + 1) * share] for i in range(4)]
    odd, up = (v & 1) == 1, (v & 2) == 2
    p, q = jnp.where(odd, b[1], b[0]), jnp.where(odd, b[0], b[1])
    r, s = jnp.where(odd, b[3], b[2]), jnp.where(odd, b[2], b[3])
    return [jnp.where(up, r, p), jnp.where(up, s, q), jnp.where(up, p, r), jnp.where(up, q, s)]


def vmem(n):
    return [pl.BlockSpec(memory_space=pltpu.VMEM)] * n


def call(kernel, outs, args, flops, out_space=pltpu.VMEM, scratch=()):
    nbytes = sum(4 * a.size for a in args) + sum(4 * o.size for o in outs)
    return pl.pallas_call(
        kernel,
        out_shape=outs,
        in_specs=vmem(len(args)),
        out_specs=[pl.BlockSpec(memory_space=out_space)] * len(outs),
        scratch_shapes=list(scratch),
        compiler_params=pltpu.CompilerParams(vmem_limit_bytes=8 * 2**20),
        cost_estimate=pl.CostEstimate(flops=flops, bytes_accessed=nbytes, transcendentals=0),
    )(*args)


def swap(a, axis, by=1):
    n = lax.axis_size(axis)
    return lax.ppermute(a, axis, [(i, i ^ by) for i in range(n)])


def gather(block):
    half = block.shape[0] // 2
    a, b = block[:half], block[half:]
    ya, xb = swap(a, "y"), swap(b, "x")
    xa, yb = swap(a, "x"), swap(b, "y")
    return a, b, xa, xb, ya, yb, swap(ya, "x"), swap(xb, "y")


def gather_factor(own):
    half, share = own.shape[0] // 2, own.shape[1]
    axes = ("core", "y", "x")
    n = lax.axis_size(axes)
    first = lax.ppermute(own, axes, [(i, i ^ (2 if i >= n // 2 else 1)) for i in range(n)])
    mine = call(cut_kernel, [jax.ShapeDtypeStruct((half, share), F32)], [first], 0)[0]
    across = lax.ppermute(mine, axes, [(i, i ^ (1 if i >= n // 2 else 2)) for i in range(n)])
    joined = call(join_kernel, [jax.ShapeDtypeStruct((half, 3 * share), F32)], [first, across], 0)[0]
    return first, across, swap(joined, "core")


def fast(vectors, reflectors, triangles):
    rows, share = vectors.shape
    panels, _, width = reflectors.shape
    sums = lax.axis_size("z")
    part = jax.ShapeDtypeStruct((share // 2, width), F32)
    whole = jax.ShapeDtypeStruct((rows, share), F32)
    work = 2 * rows * width * share
    top = panels - 1

    sections, factors = {}, {}
    for k in reversed(range(panels)):
        sections[k] = gather(reflectors[k])
        factors[k] = gather_factor(triangles[k])
        if k == top:
            pieces = list(sections[k])
            pieces[4], reflectors, triangles = lax.optimization_barrier((pieces[4], reflectors, triangles))
            sections[k] = tuple(pieces)

    def reduced(keep, send, k):
        s = keep + swap(send, "core")
        r = [swap(s, "z", by) for by in range(1, sums)]
        s = call(hold_kernel, [part], [s], 0)[0]
        mine = call(
            functools.partial(solve_kernel, k, sums), [part], [s, *r, triangles, *factors[k]], width * width * share
        )[0]
        return mine, swap(mine, "core")

    total = jax.ShapeDtypeStruct((share, width), F32)
    ahead = {k: a[:-2] for k, a in sections.items()}
    sum_so_far = call(early_kernel, [total], [vectors, *ahead[top]], work * 3 // 4)[0]
    current = vectors
    for k in reversed(range(panels)):
        keep, send = call(late_kernel, [part, part], [current, sum_so_far, *sections[k][-2:]], work // 4)
        c = reduced(keep, send, k)
        if k > 0:
            current, sum_so_far = call(
                turn_kernel, [whole, total], [current, *c, *sections[k], *ahead[k - 1]], work * 7 // 4
            )
    scratch = [pltpu.VMEM(whole.shape, F32), pltpu.SemaphoreType.DMA((PIECES,))]
    return call(last_kernel, [whole], [current, *c, *sections[0]], work, pl.ANY, scratch)[0]


def general(vectors, reflectors, triangles):
    highest = lax.Precision.HIGHEST
    row, vec = ("z", "core"), ("y", "x")
    current = vectors
    for panel in reversed(range(reflectors.shape[0])):
        section = lax.all_gather(reflectors[panel], vec, axis=0, tiled=True)
        factor = lax.all_gather(triangles[panel], vec, axis=1, tiled=True)
        partial_value = lax.dot_general(
            section, current, (((0,), (0,)), ((), ())), precision=highest, preferred_element_type=F32
        )
        share = lax.psum_scatter(partial_value, row, scatter_dimension=1, tiled=True)
        owned = jnp.dot(factor, share, precision=highest, preferred_element_type=F32)
        coefficients = lax.all_gather(owned, row, axis=1, tiled=True)
        current = current - jnp.dot(section, coefficients, precision=highest, preferred_element_type=F32)
    return current


def solution(mesh):
    rows, vecs = mesh.shape["row"], mesh.shape["vec"]
    side = next(s for s in range(int(vecs**0.5), 0, -1) if vecs % s == 0)
    cores = 2 if rows % 2 == 0 else 1
    fine = Mesh(mesh.devices.reshape(rows // cores, cores, side, vecs // side), ("z", "core", "y", "x"))
    halves = [fine.shape[axis] == 2 for axis in ("core", "y", "x")]
    small = all(halves) and fine.shape["z"] & (fine.shape["z"] - 1) == 0
    row, vec = ("z", "core"), ("y", "x")

    def body(*args):
        return (fast if small else general)(*args)

    return jax.shard_map(
        body,
        mesh=fine,
        in_specs=(P(row, vec), P(None, row + vec, None), P(None, None, vec)),
        out_specs=P(row, vec),
        check_vma=False,
    )
```

```python
import functools

import jax
import jax.numpy as jnp
from jax import lax
from jax.experimental import pallas as pl
from jax.experimental.pallas import tpu as pltpu
from jax.sharding import Mesh, PartitionSpec as P


F32, BF16 = jnp.float32, jnp.bfloat16
NN = (((1,), (0,)), ((), ()))
NT = (((1,), (1,)), ((), ()))
PIECES = 8


def split(a):
    head = a.astype(BF16)
    return head, (a - head.astype(F32)).astype(BF16)


def dot(a, b, dims):
    return lax.dot_general(a, b, dims, preferred_element_type=F32)


def stack(pair):
    return jnp.concatenate(pair, axis=0)


def dot_left(a, b, dims):
    ah, al = split(a)
    bh, bl = split(b)
    n = a.shape[0]
    both = dot(stack((ah, al)), bh, dims)
    return both[:n] + (both[n:] + dot(ah, bl, dims))


def dot_right(a, b):
    ah, al = split(a)
    n = b.shape[1] // 2
    both = dot(ah, b, NN)
    return both[:, :n] + (both[:, n:] + dot(al, b[:, :n], NN))


def place():
    return lax.axis_index("y") * 2 + lax.axis_index("x"), lax.axis_index("core")


def blocks_of(refs, skip=0):
    size = refs[0].shape[0]
    return [(i // 2, i % 2 * size, ref) for i, ref in enumerate(refs, skip)]


def window(v, block, first, size):
    return pl.ds(pl.multiple_of((v ^ block) * 2 * size + first, 8), size)


def project(current, refs, v, skip=0):
    x, r = [], []
    for block, first, ref in blocks_of(refs, skip):
        x.append(current[window(v, block, first, ref.shape[0]), :].T)
        r.append(ref[...])
    return dot_left(jnp.concatenate(x, axis=1), jnp.concatenate(r, axis=0), NN)


def give_out(total, core, keep, send):
    half = keep.shape[0]
    mine = core == 0
    keep[...] = jnp.where(mine, total[:half], total[half:])
    send[...] = jnp.where(mine, total[half:], total[:half])


def early_kernel(x, *refs):
    v, _ = place()
    refs[-1][...] = project(x, refs[:-1], v)


def late_kernel(x, total, *refs):
    v, core = place()
    refs, (keep, send) = refs[:-2], refs[-2:]
    give_out(total[...] + project(x, refs, v, PIECES - len(refs)), core, keep, send)


def coefficients(mine, other, core):
    a, b = mine[...], other[...]
    first = core == 0
    rows = jnp.concatenate([jnp.where(first, a, b), jnp.where(first, b, a)], axis=0)
    return jnp.concatenate(split(rows.T), axis=1)


def update(current, out, refs, c, v, after=None):
    for i, (block, first, ref) in enumerate(blocks_of(refs)):
        at = window(v, block, first, ref.shape[0])
        out[at, :] = current[at, :] - dot_right(ref[...], c)
        if after is not None:
            after(i, at)


def turn_kernel(x, mine, other, *refs):
    v, core = place()
    old, new, (out, total) = refs[:PIECES], refs[PIECES:-2], refs[-2:]
    update(x, out, old, coefficients(mine, other, core), v)
    total[...] = project(out, new, v)


def last_kernel(x, mine, other, *refs):
    v, core = place()
    refs, (out, made, sems) = refs[:PIECES], refs[PIECES:]
    copies = []

    def leave(i, at):
        copies.append(pltpu.make_async_copy(made.at[at, :], out.at[at, :], sems.at[i]))
        copies[-1].start()

    update(x, made, refs, coefficients(mine, other, core), v, leave)
    for copy in copies:
        copy.wait()


def cut_kernel(x, out):
    half = out.shape[0]
    out[...] = jnp.where(lax.axis_index("core") == 0, x[:half], x[half:])


def join_kernel(first, across, out):
    half, share = across.shape
    out[:, :share] = first[:half]
    out[:, share : 2 * share] = first[half:]
    out[:, 2 * share :] = across[...]


def pick_kernel(panel, x, mine, part):
    rows, half = mine.shape[0], part.shape[0]
    first = lax.axis_index("z") * rows
    mine[...] = x[panel, pl.ds(pl.multiple_of(first, 8), rows), :]
    part[...] = x[panel, pl.ds(pl.multiple_of(first + lax.axis_index("core") * half, 8), half), :]


def pack_kernel(first, across, out):
    rows = first.shape[0]
    out[:rows] = first[...]
    out[rows:] = across[...]


def spread_kernel(*refs):
    refs, out = refs[:-1], refs[-1]
    n, z = len(refs), lax.axis_index("z")
    rows = refs[0].shape[0] * 2 // 3
    for by, ref in enumerate(refs):
        at = (z ^ by) * rows
        out[pl.ds(pl.multiple_of(at, 8), rows), :] = ref[:rows]
        out[pl.ds(pl.multiple_of(n * rows + (z ^ by) * (rows // 2), 8), rows // 2), :] = ref[rows:]


def hold_kernel(x, out):
    out[...] = x[...]


def joined_blocks(first, across, exchanged, share, on_x, n):
    second = jnp.concatenate([exchanged[:, :share], exchanged[:, share : 2 * share]], axis=0)
    a, b = across[...], exchanged[:, 2 * share :]
    return first[...], second, jnp.concatenate([jnp.where(on_x, a, b), jnp.where(on_x, b, a)], axis=0)


def spread_blocks(mine, other, share, on_x, n):
    rows = mine.shape[0] * 2 // 3
    half = rows // (2 * n)
    across = []
    for at in range(rows, mine.shape[0], half):
        a, b = mine[at : at + half], other[at : at + half]
        across += [jnp.where(on_x, a, b), jnp.where(on_x, b, a)]
    return mine[:rows], other[:rows], jnp.concatenate(across, axis=0)


def solve_kernel(panel, n, *refs):
    v, core = place()
    total = refs[0][...]
    for i in range(1, n):
        total = total + refs[i][...]
    factor, *blocks, out = refs[n:]
    share = factor.shape[-1]
    on_x = core == 0
    own, along_x, along_y, far = split_columns(total, v, share)
    first, second, across = (spread_blocks if len(blocks) == 2 else joined_blocks)(*blocks, share, on_x, n)
    sums = dot_left(own, factor[panel], NT)
    sums += dot_left(jnp.where(on_x, along_x, along_y), first, NT)
    sums += dot_left(jnp.where(on_x, along_y, along_x), second, NT)
    out[...] = sums + dot_left(far, across, NT)


def split_columns(total, v, share):
    b = [total[:, i * share : (i + 1) * share] for i in range(4)]
    odd, up = (v & 1) == 1, (v & 2) == 2
    p, q = jnp.where(odd, b[1], b[0]), jnp.where(odd, b[0], b[1])
    r, s = jnp.where(odd, b[3], b[2]), jnp.where(odd, b[2], b[3])
    return [jnp.where(up, r, p), jnp.where(up, s, q), jnp.where(up, p, r), jnp.where(up, q, s)]


def vmem(n):
    return [pl.BlockSpec(memory_space=pltpu.VMEM)] * n


def call(kernel, outs, args, flops, out_space=pltpu.VMEM, scratch=()):
    nbytes = sum(4 * a.size for a in args) + sum(4 * o.size for o in outs)
    return pl.pallas_call(
        kernel,
        out_shape=outs,
        in_specs=vmem(len(args)),
        out_specs=[pl.BlockSpec(memory_space=out_space)] * len(outs),
        scratch_shapes=list(scratch),
        compiler_params=pltpu.CompilerParams(vmem_limit_bytes=8 * 2**20),
        cost_estimate=pl.CostEstimate(flops=flops, bytes_accessed=nbytes, transcendentals=0),
    )(*args)


def swap(a, axis, by=1):
    n = lax.axis_size(axis)
    return lax.ppermute(a, axis, [(i, i ^ by) for i in range(n)])


def gather(block):
    half = block.shape[0] // 2
    a, b = block[:half], block[half:]
    ya, xb = swap(a, "y"), swap(b, "x")
    xa, yb = swap(a, "x"), swap(b, "y")
    return a, b, xa, xb, ya, yb, swap(ya, "x"), swap(xb, "y")


def gather_factor(own):
    half, share = own.shape[0] // 2, own.shape[1]
    axes = ("core", "y", "x")
    n = lax.axis_size(axes)
    first = lax.ppermute(own, axes, [(i, i ^ (2 if i >= n // 2 else 1)) for i in range(n)])
    mine = call(cut_kernel, [jax.ShapeDtypeStruct((half, share), F32)], [first], 0)[0]
    across = lax.ppermute(mine, axes, [(i, i ^ (1 if i >= n // 2 else 2)) for i in range(n)])
    joined = call(join_kernel, [jax.ShapeDtypeStruct((half, 3 * share), F32)], [first, across], 0)[0]
    return first, across, swap(joined, "core")


def spread_factor(triangles, k):
    _, rows, share = triangles.shape
    axes, planes = ("core", "y", "x"), lax.axis_size("z")
    n, rows = lax.axis_size(axes), rows // planes
    shapes = [jax.ShapeDtypeStruct((r, share), F32) for r in (rows, rows // 2, rows * 3 // 2, rows * 3 // 2 * planes)]
    mine, part = call(functools.partial(pick_kernel, k), shapes[:2], [triangles], 0)
    first = lax.ppermute(mine, axes, [(i, i ^ (2 if i >= n // 2 else 1)) for i in range(n)])
    across = lax.ppermute(part, axes, [(i, i ^ 3) for i in range(n)])
    packed = call(pack_kernel, shapes[2:3], [first, across], 0)[0]
    others = [swap(packed, "z", by) for by in range(1, planes)]
    joined = call(spread_kernel, shapes[3:], [packed, *others], 0)[0]
    return joined, swap(joined, "core")


def fast(vectors, reflectors, triangles):
    rows, share = vectors.shape
    panels, _, width = reflectors.shape
    sums = lax.axis_size("z")
    part = jax.ShapeDtypeStruct((share // 2, width), F32)
    whole = jax.ShapeDtypeStruct((rows, share), F32)
    work = 2 * rows * width * share
    top = panels - 1

    sections, factors = {}, {}
    for k in reversed(range(panels)):
        sections[k] = gather(reflectors[k])
        factors[k] = spread_factor(triangles, k) if k == top else gather_factor(triangles[k])
        if k == top:
            pieces = list(sections[k])
            pieces[0], reflectors = lax.optimization_barrier((pieces[0], reflectors))
            sections[k] = tuple(pieces)

    def reduced(keep, send, k):
        s = keep + swap(send, "core")
        r = [swap(s, "z", by) for by in range(1, sums)]
        s = call(hold_kernel, [part], [s], 0)[0]
        mine = call(
            functools.partial(solve_kernel, k, sums), [part], [s, *r, triangles, *factors[k]], width * width * share
        )[0]
        return mine, swap(mine, "core")

    total = jax.ShapeDtypeStruct((share, width), F32)
    ahead = {k: a[:-2] for k, a in sections.items()}
    sum_so_far = call(early_kernel, [total], [vectors, *ahead[top]], work * 3 // 4)[0]
    current = vectors
    for k in reversed(range(panels)):
        keep, send = call(late_kernel, [part, part], [current, sum_so_far, *sections[k][-2:]], work // 4)
        c = reduced(keep, send, k)
        if k > 0:
            current, sum_so_far = call(
                turn_kernel, [whole, total], [current, *c, *sections[k], *ahead[k - 1]], work * 7 // 4
            )
    scratch = [pltpu.VMEM(whole.shape, F32), pltpu.SemaphoreType.DMA((PIECES,))]
    return call(last_kernel, [whole], [current, *c, *sections[0]], work, pl.ANY, scratch)[0]


def general(vectors, reflectors, triangles):
    highest = lax.Precision.HIGHEST
    row, vec = ("z", "core"), ("y", "x")
    current = vectors
    for panel in reversed(range(reflectors.shape[0])):
        section = lax.all_gather(reflectors[panel], vec, axis=0, tiled=True)
        factor = lax.all_gather(triangles[panel], vec, axis=1, tiled=True)
        partial_value = lax.dot_general(
            section, current, (((0,), (0,)), ((), ())), precision=highest, preferred_element_type=F32
        )
        share = lax.psum_scatter(partial_value, row, scatter_dimension=1, tiled=True)
        owned = jnp.dot(factor, share, precision=highest, preferred_element_type=F32)
        coefficients = lax.all_gather(owned, row, axis=1, tiled=True)
        current = current - jnp.dot(section, coefficients, precision=highest, preferred_element_type=F32)
    return current


def solution(mesh):
    rows, vecs = mesh.shape["row"], mesh.shape["vec"]
    side = next(s for s in range(int(vecs**0.5), 0, -1) if vecs % s == 0)
    cores = 2 if rows % 2 == 0 else 1
    fine = Mesh(mesh.devices.reshape(rows // cores, cores, side, vecs // side), ("z", "core", "y", "x"))
    halves = [fine.shape[axis] == 2 for axis in ("core", "y", "x")]
    small = all(halves) and fine.shape["z"] & (fine.shape["z"] - 1) == 0
    row, vec = ("z", "core"), ("y", "x")

    def body(*args):
        return (fast if small else general)(*args)

    return jax.shard_map(
        body,
        mesh=fine,
        in_specs=(P(row, vec), P(None, row + vec, None), P(None, None, vec)),
        out_specs=P(row, vec),
        check_vma=False,
    )
```

```python
import functools

import jax
import jax.numpy as jnp
from jax import lax
from jax.experimental import pallas as pl
from jax.experimental.pallas import tpu as pltpu
from jax.sharding import Mesh, PartitionSpec as P


F32, BF16 = jnp.float32, jnp.bfloat16
NN = (((1,), (0,)), ((), ()))
NT = (((1,), (1,)), ((), ()))
PIECES = 8


def split(a):
    head = a.astype(BF16)
    return head, (a - head.astype(F32)).astype(BF16)


def dot(a, b, dims):
    return lax.dot_general(a, b, dims, preferred_element_type=F32)


def stack(pair):
    return jnp.concatenate(pair, axis=0)


def dot_left(a, b, dims):
    ah, al = split(a)
    bh, bl = split(b)
    n = a.shape[0]
    both = dot(stack((ah, al)), bh, dims)
    return both[:n] + (both[n:] + dot(ah, bl, dims))


def dot_right(a, b):
    ah, al = split(a)
    n = b.shape[1] // 2
    both = dot(ah, b, NN)
    return both[:, :n] + (both[:, n:] + dot(al, b[:, :n], NN))


def place():
    return lax.axis_index("y") * 2 + lax.axis_index("x"), lax.axis_index("core")


def blocks_of(refs, skip=0):
    size = refs[0].shape[0]
    return [(i // 2, i % 2 * size, ref) for i, ref in enumerate(refs, skip)]


def window(v, block, first, size):
    return pl.ds(pl.multiple_of((v ^ block) * 2 * size + first, 8), size)


def project(current, refs, v, skip=0):
    x, r = [], []
    for block, first, ref in blocks_of(refs, skip):
        x.append(current[window(v, block, first, ref.shape[0]), :].T)
        r.append(ref[...])
    return dot_left(jnp.concatenate(x, axis=1), jnp.concatenate(r, axis=0), NN)


def give_out(total, core, keep, send):
    half = keep.shape[0]
    mine = core == 0
    keep[...] = jnp.where(mine, total[:half], total[half:])
    send[...] = jnp.where(mine, total[half:], total[:half])


def early_kernel(x, *refs):
    v, _ = place()
    refs[-1][...] = project(x, refs[:-1], v)


def late_kernel(x, total, *refs):
    v, core = place()
    refs, (keep, send) = refs[:-2], refs[-2:]
    give_out(total[...] + project(x, refs, v, PIECES - len(refs)), core, keep, send)


def coefficients(mine, other, core):
    a, b = mine[...], other[...]
    first = core == 0
    rows = jnp.concatenate([jnp.where(first, a, b), jnp.where(first, b, a)], axis=0)
    return jnp.concatenate(split(rows.T), axis=1)


def update(current, out, refs, c, v, after=None):
    for i, (block, first, ref) in enumerate(blocks_of(refs)):
        at = window(v, block, first, ref.shape[0])
        out[at, :] = current[at, :] - dot_right(ref[...], c)
        if after is not None:
            after(i, at)


def turn_kernel(x, mine, other, *refs):
    v, core = place()
    old, new, (out, total) = refs[:PIECES], refs[PIECES:-2], refs[-2:]
    update(x, out, old, coefficients(mine, other, core), v)
    total[...] = project(out, new, v)


def last_kernel(x, mine, other, *refs):
    v, core = place()
    refs, (out, made, sems) = refs[:PIECES], refs[PIECES:]
    copies = []

    def leave(i, at):
        copies.append(pltpu.make_async_copy(made.at[at, :], out.at[at, :], sems.at[i]))
        copies[-1].start()

    update(x, made, refs, coefficients(mine, other, core), v, leave)
    for copy in copies:
        copy.wait()


def cut_kernel(x, out):
    half = out.shape[0]
    out[...] = jnp.where(lax.axis_index("core") == 0, x[:half], x[half:])


def join_kernel(first, across, out):
    half, share = across.shape
    out[:, :share] = first[:half]
    out[:, share : 2 * share] = first[half:]
    out[:, 2 * share :] = across[...]


def pick_kernel(panel, x, mine, part):
    rows, half = mine.shape[0], part.shape[0]
    first = lax.axis_index("z") * rows
    mine[...] = x[panel, pl.ds(pl.multiple_of(first, 8), rows), :]
    part[...] = x[panel, pl.ds(pl.multiple_of(first + lax.axis_index("core") * half, 8), half), :]


def pack_kernel(first, across, out):
    rows = first.shape[0]
    out[:rows] = first[...]
    out[rows:] = across[...]


def spread_kernel(*refs):
    refs, out = refs[:-1], refs[-1]
    n, z = len(refs), lax.axis_index("z")
    rows = refs[0].shape[0] * 2 // 3
    for by, ref in enumerate(refs):
        at = (z ^ by) * rows
        out[pl.ds(pl.multiple_of(at, 8), rows), :] = ref[:rows]
        out[pl.ds(pl.multiple_of(n * rows + (z ^ by) * (rows // 2), 8), rows // 2), :] = ref[rows:]


def two_steps(planes, k, top):
    return planes == 4 and k == top


def summed(refs):
    if len(refs) != 6:
        return sum((ref[...] for ref in refs[1:]), refs[0][...])
    own, near, *far, pair, across = refs
    half = pair.shape[0]
    lower = (own[half:] + near[half:]) + (far[0][...] + far[1][...])
    return jnp.concatenate([pair[...] + across[...], lower], axis=0)


def meet_kernel(keep, received, out, low):
    total = keep[...] + received[...]
    out[...] = total
    low[...] = total[low.shape[0] :]


def pair_kernel(own, near, out):
    half = out.shape[0]
    out[...] = own[:half] + near[:half]


def hold_kernel(x, out):
    out[...] = x[...]


def joined_blocks(first, across, exchanged, share, on_x, n):
    second = jnp.concatenate([exchanged[:, :share], exchanged[:, share : 2 * share]], axis=0)
    a, b = across[...], exchanged[:, 2 * share :]
    return first[...], second, jnp.concatenate([jnp.where(on_x, a, b), jnp.where(on_x, b, a)], axis=0)


def spread_blocks(mine, other, share, on_x, n):
    rows = mine.shape[0] * 2 // 3
    half = rows // (2 * n)
    across = []
    for at in range(rows, mine.shape[0], half):
        a, b = mine[at : at + half], other[at : at + half]
        across += [jnp.where(on_x, a, b), jnp.where(on_x, b, a)]
    return mine[:rows], other[:rows], jnp.concatenate(across, axis=0)


def solve_kernel(panel, n, count, *refs):
    v, core = place()
    total = summed(refs[:count])
    factor, *blocks, out = refs[count:]
    share = factor.shape[-1]
    on_x = core == 0
    own, along_x, along_y, far = split_columns(total, v, share)
    first, second, across = (spread_blocks if len(blocks) == 2 else joined_blocks)(*blocks, share, on_x, n)
    sums = dot_left(own, factor[panel], NT)
    sums += dot_left(jnp.where(on_x, along_x, along_y), first, NT)
    sums += dot_left(jnp.where(on_x, along_y, along_x), second, NT)
    out[...] = sums + dot_left(far, across, NT)


def split_columns(total, v, share):
    b = [total[:, i * share : (i + 1) * share] for i in range(4)]
    odd, up = (v & 1) == 1, (v & 2) == 2
    p, q = jnp.where(odd, b[1], b[0]), jnp.where(odd, b[0], b[1])
    r, s = jnp.where(odd, b[3], b[2]), jnp.where(odd, b[2], b[3])
    return [jnp.where(up, r, p), jnp.where(up, s, q), jnp.where(up, p, r), jnp.where(up, q, s)]


def vmem(n):
    return [pl.BlockSpec(memory_space=pltpu.VMEM)] * n


def call(kernel, outs, args, flops, out_space=pltpu.VMEM, scratch=()):
    nbytes = sum(4 * a.size for a in args) + sum(4 * o.size for o in outs)
    return pl.pallas_call(
        kernel,
        out_shape=outs,
        in_specs=vmem(len(args)),
        out_specs=[pl.BlockSpec(memory_space=out_space)] * len(outs),
        scratch_shapes=list(scratch),
        compiler_params=pltpu.CompilerParams(vmem_limit_bytes=8 * 2**20),
        cost_estimate=pl.CostEstimate(flops=flops, bytes_accessed=nbytes, transcendentals=0),
    )(*args)


def swap(a, axis, by=1):
    n = lax.axis_size(axis)
    return lax.ppermute(a, axis, [(i, i ^ by) for i in range(n)])


def gather(block):
    half = block.shape[0] // 2
    a, b = block[:half], block[half:]
    ya, xb = swap(a, "y"), swap(b, "x")
    xa, yb = swap(a, "x"), swap(b, "y")
    return a, b, xa, xb, ya, yb, swap(ya, "x"), swap(xb, "y")


def gather_factor(own):
    half, share = own.shape[0] // 2, own.shape[1]
    axes = ("core", "y", "x")
    n = lax.axis_size(axes)
    first = lax.ppermute(own, axes, [(i, i ^ (2 if i >= n // 2 else 1)) for i in range(n)])
    mine = call(cut_kernel, [jax.ShapeDtypeStruct((half, share), F32)], [first], 0)[0]
    across = lax.ppermute(mine, axes, [(i, i ^ (1 if i >= n // 2 else 2)) for i in range(n)])
    joined = call(join_kernel, [jax.ShapeDtypeStruct((half, 3 * share), F32)], [first, across], 0)[0]
    return first, across, swap(joined, "core")


def spread_factor(triangles, k):
    _, rows, share = triangles.shape
    axes, planes = ("core", "y", "x"), lax.axis_size("z")
    n, rows = lax.axis_size(axes), rows // planes
    shapes = [jax.ShapeDtypeStruct((r, share), F32) for r in (rows, rows // 2, rows * 3 // 2, rows * 3 // 2 * planes)]
    mine, part = call(functools.partial(pick_kernel, k), shapes[:2], [triangles], 0)
    first = lax.ppermute(mine, axes, [(i, i ^ (2 if i >= n // 2 else 1)) for i in range(n)])
    across = lax.ppermute(part, axes, [(i, i ^ 3) for i in range(n)])
    packed = call(pack_kernel, shapes[2:3], [first, across], 0)[0]
    others = [swap(packed, "z", by) for by in range(1, planes)]
    joined = call(spread_kernel, shapes[3:], [packed, *others], 0)[0]
    return joined, swap(joined, "core")


def fast(vectors, reflectors, triangles):
    rows, share = vectors.shape
    panels, _, width = reflectors.shape
    sums = lax.axis_size("z")
    part = jax.ShapeDtypeStruct((share // 2, width), F32)
    whole = jax.ShapeDtypeStruct((rows, share), F32)
    work = 2 * rows * width * share
    top = panels - 1

    sections, factors = {}, {}
    for k in reversed(range(panels)):
        sections[k] = gather(reflectors[k])
        factors[k] = spread_factor(triangles, k) if k == top else gather_factor(triangles[k])
        if k == top:
            pieces = list(sections[k])
            pieces[0], reflectors = lax.optimization_barrier((pieces[0], reflectors))
            sections[k] = tuple(pieces)

    def reduced(keep, send, k):
        received = swap(send, "core")
        if two_steps(sums, k, top):
            piece = jax.ShapeDtypeStruct((share // 4, width), F32)
            s, low = call(meet_kernel, [part, piece], [keep, received], 0)
            r = [swap(s, "z", 1), swap(low, "z", 2), swap(low, "z", 3)]
            pair = call(pair_kernel, [piece], [s, r[0]], 0)[0]
            r += [pair, swap(pair, "z", 2)]
        else:
            s = keep + received
            r = [swap(s, "z", by) for by in range(1, sums)]
        s = call(hold_kernel, [part], [s], 0)[0]
        mine = call(
            functools.partial(solve_kernel, k, sums, 1 + len(r)),
            [part],
            [s, *r, triangles, *factors[k]],
            width * width * share,
        )[0]
        return mine, swap(mine, "core")

    total = jax.ShapeDtypeStruct((share, width), F32)
    ahead = {k: a[:-2] for k, a in sections.items()}
    sum_so_far = call(early_kernel, [total], [vectors, *ahead[top]], work * 3 // 4)[0]
    current = vectors
    for k in reversed(range(panels)):
        keep, send = call(late_kernel, [part, part], [current, sum_so_far, *sections[k][-2:]], work // 4)
        c = reduced(keep, send, k)
        if k > 0:
            current, sum_so_far = call(
                turn_kernel, [whole, total], [current, *c, *sections[k], *ahead[k - 1]], work * 7 // 4
            )
    scratch = [pltpu.VMEM(whole.shape, F32), pltpu.SemaphoreType.DMA((PIECES,))]
    return call(last_kernel, [whole], [current, *c, *sections[0]], work, pl.ANY, scratch)[0]


def general(vectors, reflectors, triangles):
    highest = lax.Precision.HIGHEST
    row, vec = ("z", "core"), ("y", "x")
    current = vectors
    for panel in reversed(range(reflectors.shape[0])):
        section = lax.all_gather(reflectors[panel], vec, axis=0, tiled=True)
        factor = lax.all_gather(triangles[panel], vec, axis=1, tiled=True)
        partial_value = lax.dot_general(
            section, current, (((0,), (0,)), ((), ())), precision=highest, preferred_element_type=F32
        )
        share = lax.psum_scatter(partial_value, row, scatter_dimension=1, tiled=True)
        owned = jnp.dot(factor, share, precision=highest, preferred_element_type=F32)
        coefficients = lax.all_gather(owned, row, axis=1, tiled=True)
        current = current - jnp.dot(section, coefficients, precision=highest, preferred_element_type=F32)
    return current


def solution(mesh):
    rows, vecs = mesh.shape["row"], mesh.shape["vec"]
    side = next(s for s in range(int(vecs**0.5), 0, -1) if vecs % s == 0)
    cores = 2 if rows % 2 == 0 else 1
    fine = Mesh(mesh.devices.reshape(rows // cores, cores, side, vecs // side), ("z", "core", "y", "x"))
    halves = [fine.shape[axis] == 2 for axis in ("core", "y", "x")]
    small = all(halves) and fine.shape["z"] & (fine.shape["z"] - 1) == 0
    row, vec = ("z", "core"), ("y", "x")

    def body(*args):
        return (fast if small else general)(*args)

    return jax.shard_map(
        body,
        mesh=fine,
        in_specs=(P(row, vec), P(None, row + vec, None), P(None, None, vec)),
        out_specs=P(row, vec),
        check_vma=False,
    )
```

```python
import functools

import jax
import jax.numpy as jnp
from jax import lax
from jax.experimental import pallas as pl
from jax.experimental.pallas import tpu as pltpu
from jax.sharding import Mesh, PartitionSpec as P


F32, BF16 = jnp.float32, jnp.bfloat16
NN = (((1,), (0,)), ((), ()))
NT = (((1,), (1,)), ((), ()))
PIECES = 8


def split(a):
    head = a.astype(BF16)
    return head, (a - head.astype(F32)).astype(BF16)


def dot(a, b, dims):
    return lax.dot_general(a, b, dims, preferred_element_type=F32)


def stack(pair):
    return jnp.concatenate(pair, axis=0)


def dot_left(a, b, dims):
    ah, al = split(a)
    bh, bl = split(b)
    n = a.shape[0]
    both = dot(stack((ah, al)), bh, dims)
    return both[:n] + (both[n:] + dot(ah, bl, dims))


def dot_right(a, b):
    ah, al = split(a)
    n = b.shape[1] // 2
    both = dot(ah, b, NN)
    return both[:, :n] + (both[:, n:] + dot(al, b[:, :n], NN))


def place():
    return lax.axis_index("y") * 2 + lax.axis_index("x"), lax.axis_index("core")


def blocks_of(refs, skip=0):
    size = refs[0].shape[0]
    return [(i // 2, i % 2 * size, ref) for i, ref in enumerate(refs, skip)]


def window(v, block, first, size):
    return pl.ds(pl.multiple_of((v ^ block) * 2 * size + first, 8), size)


def project(current, refs, v, skip=0):
    x, r = [], []
    for block, first, ref in blocks_of(refs, skip):
        x.append(current[window(v, block, first, ref.shape[0]), :].T)
        r.append(ref[...])
    return dot_left(jnp.concatenate(x, axis=1), jnp.concatenate(r, axis=0), NN)


def give_out(total, core, keep, send):
    half = keep.shape[0]
    mine = core == 0
    keep[...] = jnp.where(mine, total[:half], total[half:])
    send[...] = jnp.where(mine, total[half:], total[:half])


def early_kernel(x, *refs):
    v, _ = place()
    refs[-1][...] = project(x, refs[:-1], v)


def late_kernel(x, total, *refs):
    v, core = place()
    refs, (keep, send) = refs[:-2], refs[-2:]
    give_out(total[...] + project(x, refs, v, PIECES - len(refs)), core, keep, send)


def coefficients(mine, other, core):
    a, b = mine[...], other[...]
    first = core == 0
    rows = jnp.concatenate([jnp.where(first, a, b), jnp.where(first, b, a)], axis=0)
    return jnp.concatenate(split(rows.T), axis=1)


def update(current, out, refs, c, v, after=None):
    for i, (block, first, ref) in enumerate(blocks_of(refs)):
        at = window(v, block, first, ref.shape[0])
        out[at, :] = current[at, :] - dot_right(ref[...], c)
        if after is not None:
            after(i, at)


def turn_kernel(x, mine, other, *refs):
    v, core = place()
    old, new, (out, total) = refs[:PIECES], refs[PIECES:-2], refs[-2:]
    update(x, out, old, coefficients(mine, other, core), v)
    total[...] = project(out, new, v)


def last_kernel(x, mine, other, *refs):
    v, core = place()
    refs, (out, made, sems) = refs[:PIECES], refs[PIECES:]
    copies = []

    def leave(i, at):
        copies.append(pltpu.make_async_copy(made.at[at, :], out.at[at, :], sems.at[i]))
        copies[-1].start()

    update(x, made, refs, coefficients(mine, other, core), v, leave)
    for copy in copies:
        copy.wait()


def cut_kernel(x, out):
    half = out.shape[0]
    out[...] = jnp.where(lax.axis_index("core") == 0, x[:half], x[half:])


def join_kernel(first, across, out):
    half, share = across.shape
    out[:, :share] = first[:half]
    out[:, share : 2 * share] = first[half:]
    out[:, 2 * share :] = across[...]


def pick_kernel(panel, x, mine, part):
    rows, half = mine.shape[0], part.shape[0]
    first = lax.axis_index("z") * rows
    mine[...] = x[panel, pl.ds(pl.multiple_of(first, 8), rows), :]
    part[...] = x[panel, pl.ds(pl.multiple_of(first + lax.axis_index("core") * half, 8), half), :]


def pack_kernel(first, across, out):
    rows = first.shape[0]
    out[:rows] = first[...]
    out[rows:] = across[...]


def spread_kernel(*refs):
    refs, out = refs[:-1], refs[-1]
    n, z = len(refs), lax.axis_index("z")
    rows = refs[0].shape[0] * 2 // 3
    for by, ref in enumerate(refs):
        at = (z ^ by) * rows
        out[pl.ds(pl.multiple_of(at, 8), rows), :] = ref[:rows]
        out[pl.ds(pl.multiple_of(n * rows + (z ^ by) * (rows // 2), 8), rows // 2), :] = ref[rows:]


def two_steps(planes, k):
    return planes == 4 and k == 0


def summed(refs):
    if len(refs) != 6:
        return sum((ref[...] for ref in refs[1:]), refs[0][...])
    own, near, *far, pair, across = refs
    half = pair.shape[0]
    lower = (own[half:] + near[half:]) + (far[0][...] + far[1][...])
    return jnp.concatenate([pair[...] + across[...], lower], axis=0)


def meet_kernel(keep, received, out, low):
    total = keep[...] + received[...]
    out[...] = total
    low[...] = total[low.shape[0] :]


def pair_kernel(own, near, out):
    half = out.shape[0]
    out[...] = own[:half] + near[:half]


def hold_kernel(x, out):
    out[...] = x[...]


def joined_blocks(first, across, exchanged, share, on_x, n):
    second = jnp.concatenate([exchanged[:, :share], exchanged[:, share : 2 * share]], axis=0)
    a, b = across[...], exchanged[:, 2 * share :]
    return first[...], second, jnp.concatenate([jnp.where(on_x, a, b), jnp.where(on_x, b, a)], axis=0)


def spread_blocks(mine, other, share, on_x, n):
    rows = mine.shape[0] * 2 // 3
    half = rows // (2 * n)
    across = []
    for at in range(rows, mine.shape[0], half):
        a, b = mine[at : at + half], other[at : at + half]
        across += [jnp.where(on_x, a, b), jnp.where(on_x, b, a)]
    return mine[:rows], other[:rows], jnp.concatenate(across, axis=0)


def solve_kernel(panel, n, count, *refs):
    v, core = place()
    total = summed(refs[:count])
    factor, *blocks, out = refs[count:]
    share = factor.shape[-1]
    on_x = core == 0
    own, along_x, along_y, far = split_columns(total, v, share)
    first, second, across = (spread_blocks if len(blocks) == 2 else joined_blocks)(*blocks, share, on_x, n)
    sums = dot_left(own, factor[panel], NT)
    sums += dot_left(jnp.where(on_x, along_x, along_y), first, NT)
    sums += dot_left(jnp.where(on_x, along_y, along_x), second, NT)
    out[...] = sums + dot_left(far, across, NT)


def split_columns(total, v, share):
    b = [total[:, i * share : (i + 1) * share] for i in range(4)]
    odd, up = (v & 1) == 1, (v & 2) == 2
    p, q = jnp.where(odd, b[1], b[0]), jnp.where(odd, b[0], b[1])
    r, s = jnp.where(odd, b[3], b[2]), jnp.where(odd, b[2], b[3])
    return [jnp.where(up, r, p), jnp.where(up, s, q), jnp.where(up, p, r), jnp.where(up, q, s)]


def vmem(n):
    return [pl.BlockSpec(memory_space=pltpu.VMEM)] * n


def call(kernel, outs, args, flops, out_space=pltpu.VMEM, scratch=()):
    nbytes = sum(4 * a.size for a in args) + sum(4 * o.size for o in outs)
    return pl.pallas_call(
        kernel,
        out_shape=outs,
        in_specs=vmem(len(args)),
        out_specs=[pl.BlockSpec(memory_space=out_space)] * len(outs),
        scratch_shapes=list(scratch),
        compiler_params=pltpu.CompilerParams(vmem_limit_bytes=8 * 2**20),
        cost_estimate=pl.CostEstimate(flops=flops, bytes_accessed=nbytes, transcendentals=0),
    )(*args)


def swap(a, axis, by=1):
    n = lax.axis_size(axis)
    return lax.ppermute(a, axis, [(i, i ^ by) for i in range(n)])


def gather(block):
    half = block.shape[0] // 2
    a, b = block[:half], block[half:]
    ya, xb = swap(a, "y"), swap(b, "x")
    xa, yb = swap(a, "x"), swap(b, "y")
    return a, b, xa, xb, ya, yb, swap(ya, "x"), swap(xb, "y")


def gather_factor(own):
    half, share = own.shape[0] // 2, own.shape[1]
    axes = ("core", "y", "x")
    n = lax.axis_size(axes)
    first = lax.ppermute(own, axes, [(i, i ^ (2 if i >= n // 2 else 1)) for i in range(n)])
    mine = call(cut_kernel, [jax.ShapeDtypeStruct((half, share), F32)], [first], 0)[0]
    across = lax.ppermute(mine, axes, [(i, i ^ (1 if i >= n // 2 else 2)) for i in range(n)])
    joined = call(join_kernel, [jax.ShapeDtypeStruct((half, 3 * share), F32)], [first, across], 0)[0]
    return first, across, swap(joined, "core")


def spread_factor(triangles, k):
    _, rows, share = triangles.shape
    axes, planes = ("core", "y", "x"), lax.axis_size("z")
    n, rows = lax.axis_size(axes), rows // planes
    shapes = [jax.ShapeDtypeStruct((r, share), F32) for r in (rows, rows // 2, rows * 3 // 2, rows * 3 // 2 * planes)]
    mine, part = call(functools.partial(pick_kernel, k), shapes[:2], [triangles], 0)
    first = lax.ppermute(mine, axes, [(i, i ^ (2 if i >= n // 2 else 1)) for i in range(n)])
    across = lax.ppermute(part, axes, [(i, i ^ 3) for i in range(n)])
    packed = call(pack_kernel, shapes[2:3], [first, across], 0)[0]
    others = [swap(packed, "z", by) for by in range(1, planes)]
    joined = call(spread_kernel, shapes[3:], [packed, *others], 0)[0]
    return joined, swap(joined, "core")


def fast(vectors, reflectors, triangles):
    rows, share = vectors.shape
    panels, _, width = reflectors.shape
    sums = lax.axis_size("z")
    part = jax.ShapeDtypeStruct((share // 2, width), F32)
    whole = jax.ShapeDtypeStruct((rows, share), F32)
    work = 2 * rows * width * share
    top = panels - 1

    sections, factors = {}, {}
    for k in reversed(range(panels)):
        sections[k] = gather(reflectors[k])
        factors[k] = spread_factor(triangles, k) if k == top else gather_factor(triangles[k])
        if k == top:
            pieces = list(sections[k])
            pieces[0], reflectors = lax.optimization_barrier((pieces[0], reflectors))
            sections[k] = tuple(pieces)

    def reduced(keep, send, k):
        received = swap(send, "core")
        if two_steps(sums, k):
            piece = jax.ShapeDtypeStruct((share // 4, width), F32)
            s, low = call(meet_kernel, [part, piece], [keep, received], 0)
            r = [swap(s, "z", 1), swap(low, "z", 2), swap(low, "z", 3)]
            pair = call(pair_kernel, [piece], [s, r[0]], 0)[0]
            r += [pair, swap(pair, "z", 2)]
        else:
            s = keep + received
            r = [swap(s, "z", by) for by in range(1, sums)]
        s = call(hold_kernel, [part], [s], 0)[0]
        mine = call(
            functools.partial(solve_kernel, k, sums, 1 + len(r)),
            [part],
            [s, *r, triangles, *factors[k]],
            width * width * share,
        )[0]
        return mine, swap(mine, "core")

    total = jax.ShapeDtypeStruct((share, width), F32)
    ahead = {k: a[:-2] for k, a in sections.items()}
    sum_so_far = call(early_kernel, [total], [vectors, *ahead[top]], work * 3 // 4)[0]
    current = vectors
    for k in reversed(range(panels)):
        keep, send = call(late_kernel, [part, part], [current, sum_so_far, *sections[k][-2:]], work // 4)
        c = reduced(keep, send, k)
        if k > 0:
            current, sum_so_far = call(
                turn_kernel, [whole, total], [current, *c, *sections[k], *ahead[k - 1]], work * 7 // 4
            )
    scratch = [pltpu.VMEM(whole.shape, F32), pltpu.SemaphoreType.DMA((PIECES,))]
    return call(last_kernel, [whole], [current, *c, *sections[0]], work, pl.ANY, scratch)[0]


def general(vectors, reflectors, triangles):
    highest = lax.Precision.HIGHEST
    row, vec = ("z", "core"), ("y", "x")
    current = vectors
    for panel in reversed(range(reflectors.shape[0])):
        section = lax.all_gather(reflectors[panel], vec, axis=0, tiled=True)
        factor = lax.all_gather(triangles[panel], vec, axis=1, tiled=True)
        partial_value = lax.dot_general(
            section, current, (((0,), (0,)), ((), ())), precision=highest, preferred_element_type=F32
        )
        share = lax.psum_scatter(partial_value, row, scatter_dimension=1, tiled=True)
        owned = jnp.dot(factor, share, precision=highest, preferred_element_type=F32)
        coefficients = lax.all_gather(owned, row, axis=1, tiled=True)
        current = current - jnp.dot(section, coefficients, precision=highest, preferred_element_type=F32)
    return current


def solution(mesh):
    rows, vecs = mesh.shape["row"], mesh.shape["vec"]
    side = next(s for s in range(int(vecs**0.5), 0, -1) if vecs % s == 0)
    cores = 2 if rows % 2 == 0 else 1
    fine = Mesh(mesh.devices.reshape(rows // cores, cores, side, vecs // side), ("z", "core", "y", "x"))
    halves = [fine.shape[axis] == 2 for axis in ("core", "y", "x")]
    small = all(halves) and fine.shape["z"] & (fine.shape["z"] - 1) == 0
    row, vec = ("z", "core"), ("y", "x")

    def body(*args):
        return (fast if small else general)(*args)

    return jax.shard_map(
        body,
        mesh=fine,
        in_specs=(P(row, vec), P(None, row + vec, None), P(None, None, vec)),
        out_specs=P(row, vec),
        check_vma=False,
    )
```
